32 devices in a mesh: tp: 2 (over x), dp: 16 (over z, y, core).
Axes of the slice: x: 2, y: 2, z: 4, core: 2. Of those that a mesh axis runs over, the one named last changes fastest.
Arguments:
- layer_input: bfloat16 [2, 16, 64, 2048], P(None, 'dp', 'tp'), may hold values from -6 to 6
- query_weight: bfloat16 [2048, 2048], P('dp', 'tp'), may hold values from -0.125 to 0.125
- key_matrix: bfloat16 [2048, 1024], P('dp', 'tp'), may hold values from -0.125 to 0.125
- value_matrix: bfloat16 [2048, 1024], P('dp', 'tp'), may hold values from -0.125 to 0.125
- output_weight: bfloat16 [2048, 2048], P('tp', 'dp'), may hold values from -2 to 2
- gate_weight: bfloat16 [2048, 6144], P('dp', 'tp'), may hold values from -0.125 to 0.125
- up_weight: bfloat16 [2048, 6144], P('dp', 'tp'), may hold values from -0.125 to 0.125
- down_weight: bfloat16 [6144, 2048], P('tp', 'dp'), may hold values from -0.078125 to 0.078125
- attn_gain: float32 [2048], replicated, may hold values from 0.1 to 1.9
- mlp_gain: float32 [2048], replicated, may hold values from 0.1 to 1.9
- query_gain: float32 [128], replicated, may hold values from 0.8 to 1.8
- key_gain: float32 [128], replicated, may hold values from 0.8 to 1.8
- cotangent: bfloat16 [2, 16, 64, 2048], P(None, 'dp', 'tp'), may hold values from -6 to 6
Outputs:
- layer_output: bfloat16 [2, 16, 64, 2048], P(None, 'dp', 'tp')
- input_grad: bfloat16 [2, 16, 64, 2048], P(None, 'dp', 'tp')
- query_grad: float32 [2048, 2048], P('dp', 'tp')
- key_grad: float32 [2048, 1024], P('dp', 'tp')
- value_grad: float32 [2048, 1024], P('dp', 'tp')
- output_grad: float32 [2048, 2048], P('tp', 'dp')
- gate_grad: float32 [2048, 6144], P('dp', 'tp')
- up_grad: float32 [2048, 6144], P('dp', 'tp')
- down_grad: float32 [6144, 2048], P('tp', 'dp')
- attn_gain_grad: float32 [2048], replicated
- mlp_gain_grad: float32 [2048], replicated
- query_gain_grad: float32 [128], replicated
- key_gain_grad: float32 [128], replicated
The draws below stay inside these ranges and needn't reach their ends.
All inputs are finite; a program needn't handle non-finite values.
Results may differ from the reference program's by a relative error of at most 0.018.
Values may be sent and summed in bfloat16 or wider, within the bound.
No kernel may reach another device: no remote copies, remote signals or barrier semaphores. Data moves between devices by JAX's collectives and lax.ppermute only.
A program may use at most 448 MiB of HBM per device.

```python
import jax
import jax.numpy as jnp
from jax import lax

MODEL_WIDTH = 2048
HQ = 16
KEY_HEADS = 8
HEAD_SIZE = 128
FF = 6144
ROWS_DEV = 64
SEGMENTS = 2
SCORE_BLOCK_ROWS = 512
BLOCKS = 16
SEQUENCE_TOKENS = 2048
QUERY_GROUP = 2


def level_of(key, dims, shards, smallest, largest):
    gain, own = 1.0, jax.random.fold_in(key, 6)
    for axis_at, parts in shards:
        steps = jnp.exp(jax.random.uniform(jax.random.fold_in(own, axis_at), (parts,), jnp.float32, smallest / len(shards), largest / len(shards)))
        gain = gain * jnp.repeat(steps, dims[axis_at] // parts).reshape([-1 if axis == axis_at else 1 for axis in range(len(dims))])
    return gain


def gaussian(stream_key, extent, scale, reach, split=(), held_as=jnp.bfloat16):
    level = level_of(stream_key, extent, split, -0.22, 0.18) if split else 1.0
    values = jax.random.normal(stream_key, extent, jnp.float32) * scale * level
    return jnp.minimum(jnp.maximum(values, -reach), reach).astype(held_as)


def setup_inputs(seed: int = 0) -> dict:
    key_of = jax.random.split(jax.random.key(seed), 14)
    layer_input = gaussian(key_of[0], (SEGMENTS, BLOCKS, ROWS_DEV, MODEL_WIDTH), 1.0, 6.0, ((1, 16), (2, 2)))
    query_weight = gaussian(key_of[1], (MODEL_WIDTH, HQ * HEAD_SIZE), MODEL_WIDTH ** -0.5, 0.125, ((0, 16), (1, 2)))
    key_matrix = gaussian(key_of[2], (MODEL_WIDTH, KEY_HEADS * HEAD_SIZE), MODEL_WIDTH ** -0.5, 0.125, ((0, 16), (1, 2)))
    value_matrix = gaussian(key_of[3], (MODEL_WIDTH, KEY_HEADS * HEAD_SIZE), MODEL_WIDTH ** -0.5, 0.125, ((0, 16), (1, 2)))
    output_weight = gaussian(key_of[4], (HQ * HEAD_SIZE, MODEL_WIDTH), (max(HQ * HEAD_SIZE // 256, 1)) ** -0.5, 2.0, ((0, 2), (1, 16)))
    gate_weight = gaussian(key_of[5], (MODEL_WIDTH, FF), MODEL_WIDTH ** -0.5, 0.125, ((0, 16), (1, 2)))
    up_weight = gaussian(key_of[6], (MODEL_WIDTH, FF), MODEL_WIDTH ** -0.5, 0.125, ((0, 16), (1, 2)))
    down_weight = gaussian(key_of[7], (FF, MODEL_WIDTH), FF ** -0.5, 0.078125, ((0, 2), (1, 16)))
    attn_gain = jnp.clip(1.0 + 0.18 * jax.random.normal(key_of[8], (MODEL_WIDTH,), jnp.float32), 0.1, 1.9)
    mlp_gain = jnp.clip(1.0 + 0.18 * jax.random.normal(key_of[9], (MODEL_WIDTH,), jnp.float32), 0.1, 1.9)
    query_gain = jnp.clip(jax.random.uniform(key_of[10], (HEAD_SIZE,), jnp.float32, 0.8, 1.8), 0.8, 1.8)
    key_gain = jnp.clip(jax.random.uniform(key_of[11], (HEAD_SIZE,), jnp.float32, 0.8, 1.8), 0.8, 1.8)
    cotangent = gaussian(key_of[12], (SEGMENTS, BLOCKS, ROWS_DEV, MODEL_WIDTH), 1.0, 6.0, ((1, 16), (2, 2)))
    return {"layer_input": layer_input, "query_weight": query_weight, "key_matrix": key_matrix, "value_matrix": value_matrix, "output_weight": output_weight, "gate_weight": gate_weight, "up_weight": up_weight, "down_weight": down_weight, "attn_gain": attn_gain, "mlp_gain": mlp_gain, "query_gain": query_gain, "key_gain": key_gain, "cotangent": cotangent}


@jax.custom_vjp
def lower_precision(v):
    return lax.optimization_barrier(v.astype(jnp.bfloat16)).astype(jnp.float32)

@jax.custom_vjp
def lower_backward(v):
    return v

def low_keep(v):
    return (lower_precision(v), None)

def low_pass(kept, grad):
    return (grad,)

def back_keep(v):
    return (v, None)

def back_low(kept, grad):
    return (lower_precision(grad),)
lower_precision.defvjp(low_keep, low_pass)
lower_backward.defvjp(back_keep, back_low)
EPSILON = 1e-06
ROPE_BASE = 1000000.0
MASKED = -1e+30
EXACT_PRECISION = lax.Precision.HIGHEST

def norm_rows(value_rows, gain_vec):
    return value_rows * lax.rsqrt(lax.optimization_barrier(jnp.mean(value_rows * value_rows, axis=-1, keepdims=True)) + EPSILON) * gain_vec

def rotate(value_rows, cosine_table, sine_table):
    half_width = value_rows.shape[-1] // 2
    turned = jnp.concatenate([-value_rows[..., half_width:], value_rows[..., :half_width]], axis=-1)
    return value_rows * cosine_table + turned * sine_table

def tables(positions, head_width):
    half_width = head_width // 2
    inverse = ROPE_BASE ** (-(jnp.arange(half_width, dtype=jnp.float32) * 2.0 / head_width))
    angles = positions.astype(jnp.float32)[:, None] * inverse[None, :]
    angles = jnp.concatenate([angles, angles], axis=-1)[:, None, :]
    return (jnp.cos(angles), jnp.sin(angles))

def attention(query_rows, key_rows, value_rows):
    block_list = SEQUENCE_TOKENS // SCORE_BLOCK_ROWS
    grouped_heads = query_rows.reshape(block_list, SCORE_BLOCK_ROWS, KEY_HEADS, QUERY_GROUP, HEAD_SIZE)
    starts = jnp.arange(block_list, dtype=jnp.int32) * SCORE_BLOCK_ROWS
    key_pos = jnp.arange(SEQUENCE_TOKENS, dtype=jnp.int32)

    def one_block(query_block, offset):
        raw_scores = jnp.einsum('qkgd,skd->kgqs', query_block, key_rows, precision=EXACT_PRECISION) * HEAD_SIZE ** (-0.5)
        scores = lower_backward(raw_scores)
        query_pos = offset + jnp.arange(SCORE_BLOCK_ROWS, dtype=jnp.int32)
        scores = jnp.where(key_pos[None, :] <= query_pos[:, None], scores, MASKED)
        highest = lax.optimization_barrier(jnp.max(scores, axis=-1, keepdims=True))
        log_total = highest + jnp.log(lax.optimization_barrier(jnp.sum(jnp.exp(scores - highest), axis=-1, keepdims=True)))
        prob_rows = lower_precision(jnp.exp(scores - log_total))
        attended = jnp.einsum('kgqs,skd->qkgd', prob_rows, value_rows, precision=EXACT_PRECISION)
        return lower_backward(lower_precision(attended)).reshape(SCORE_BLOCK_ROWS, HQ * HEAD_SIZE)
    checked = jax.checkpoint(one_block)
    results = lax.map(lambda paired: checked(paired[0], paired[1]), (grouped_heads, starts))
    return results.reshape(SEQUENCE_TOKENS, HQ * HEAD_SIZE)

def forward(flat_rows, query_weight, key_matrix, value_matrix, output_weight, gate_weight, up_weight, down_weight, attn_gain, mlp_gain, query_gain, key_gain):
    positions = jnp.arange(SEQUENCE_TOKENS, dtype=jnp.int32)
    cosine_table, sine_table = tables(positions, HEAD_SIZE)
    normalized_rows = lower_precision(norm_rows(flat_rows, attn_gain))
    q_raw = lower_backward(jnp.dot(normalized_rows, query_weight, precision=EXACT_PRECISION)).reshape(SEQUENCE_TOKENS, HQ, HEAD_SIZE)
    key_unrotated = lower_backward(jnp.dot(normalized_rows, key_matrix, precision=EXACT_PRECISION)).reshape(SEQUENCE_TOKENS, KEY_HEADS, HEAD_SIZE)
    value_rows = lower_precision(lower_backward(jnp.dot(normalized_rows, value_matrix, precision=EXACT_PRECISION))).reshape(SEQUENCE_TOKENS, KEY_HEADS, HEAD_SIZE)
    query_rows = lower_precision(rotate(norm_rows(q_raw, query_gain), cosine_table, sine_table))
    key_rows = lower_precision(rotate(norm_rows(key_unrotated, key_gain), cosine_table, sine_table))
    head_out = attention(query_rows, key_rows, value_rows)
    middle = flat_rows + lower_backward(jnp.dot(head_out, output_weight, precision=EXACT_PRECISION))
    normed2 = lower_precision(norm_rows(middle, mlp_gain))
    gate_pre = lower_backward(jnp.dot(normed2, gate_weight, precision=EXACT_PRECISION))
    up_pre = lower_backward(jnp.dot(normed2, up_weight, precision=EXACT_PRECISION))
    active = lower_precision(jax.nn.silu(gate_pre) * up_pre)
    return middle + lower_backward(jnp.dot(active, down_weight, precision=EXACT_PRECISION))

def reference(layer_input, query_weight, key_matrix, value_matrix, output_weight, gate_weight, up_weight, down_weight, attn_gain, mlp_gain, query_gain, key_gain, cotangent):
    whole_shape = layer_input.shape
    floats = [item.astype(jnp.float32) for item in (layer_input.reshape(SEQUENCE_TOKENS, MODEL_WIDTH), query_weight, key_matrix, value_matrix, output_weight, gate_weight, up_weight, down_weight, attn_gain, mlp_gain, query_gain, key_gain)]
    result, pull_back = jax.vjp(forward, *floats)
    gradients = pull_back(cotangent.reshape(SEQUENCE_TOKENS, MODEL_WIDTH).astype(jnp.float32))
    return (result.astype(jnp.bfloat16).reshape(whole_shape), gradients[0].astype(jnp.bfloat16).reshape(whole_shape), gradients[1], gradients[2], gradients[3], gradients[4], gradients[5], gradients[6], gradients[7], gradients[8], gradients[9], gradients[10], gradients[11])
```

```python
import functools

import jax
import jax.numpy as jnp
from jax import lax
from jax.experimental import pallas as pl
from jax.experimental.pallas import tpu as pltpu
from jax.sharding import PartitionSpec as P

HEAD_SIZE = 128
ROWS_DEV = 64

EPSILON = 1e-06
ROPE_BASE = 1000000.0
MASKED = -1e30

CORE = 1
SPLIT = 8

BF = jnp.bfloat16
F32 = jnp.float32


def norm_rows(value_rows, gain_vec):
    return (
        value_rows
        * lax.rsqrt(jnp.mean(value_rows * value_rows, axis=-1, keepdims=True) + EPSILON)
        * gain_vec
    )


def rotate(value_rows, cosine_table, sine_table):
    half_width = value_rows.shape[-1] // 2
    turned = jnp.concatenate([-value_rows[..., half_width:], value_rows[..., :half_width]], axis=-1)
    return value_rows * cosine_table + turned * sine_table


def tables(positions, head_width):
    half_width = head_width // 2
    inverse = ROPE_BASE ** (-(jnp.arange(half_width, dtype=F32) * 2.0 / head_width))
    angles = positions.astype(F32)[:, None] * inverse[None, :]
    angles = jnp.concatenate([angles, angles], axis=-1)
    return (jnp.cos(angles), jnp.sin(angles))


def dot(left, right):
    return jnp.dot(left, right, preferred_element_type=F32)


def dot_nt(left, right):
    return lax.dot_general(left, right, (((1,), (1,)), ((), ())), preferred_element_type=F32)


def dot_tn(left, right):
    return lax.dot_general(left, right, (((0,), (0,)), ((), ())), preferred_element_type=F32)


def stack_heads(ref, segment):
    value = ref[:, segment]
    rows = value.shape[0] * value.shape[1]
    return jnp.concatenate(
        [
            value[:, :, h : h + HEAD_SIZE].reshape(rows, HEAD_SIZE)
            for h in range(0, value.shape[2], HEAD_SIZE)
        ],
        axis=0,
    )


def unstack_heads(ref, segment, value):
    rows = ref.shape[0] * ref.shape[2]
    for h in range(ref.shape[3] // HEAD_SIZE):
        block = value[h * rows : (h + 1) * rows]
        ref[:, segment, :, h * HEAD_SIZE : (h + 1) * HEAD_SIZE] = block.reshape(
            ref.shape[0], ref.shape[2], HEAD_SIZE
        )


def attend_kernel(scale, q_ref, kv_ref, qpos_ref, kpos_ref, out_ref, lse_ref):
    groups, _, segments, half, wide = kv_ref.shape
    rows = 2 * half
    for segment in range(segments):
        q = stack_heads(q_ref, segment)
        qpos = qpos_ref[segment]
        qpos = jnp.concatenate([qpos] * (q.shape[0] // rows), axis=0)

        def step(index, carry, q=q, qpos=qpos):
            high, total, acc = carry
            part = lax.div(index, groups)
            block = kv_ref[lax.rem(index, groups), :, part].reshape(rows, wide)
            scores = dot_nt(q, block[:, :HEAD_SIZE]) * scale
            scores = jnp.where(kpos_ref[index] <= qpos, scores, MASKED)
            top = jnp.maximum(high, jnp.max(scores, axis=-1, keepdims=True))
            shrink = jnp.exp(high - top)
            probs = jnp.exp(scores - top)
            total = total * shrink + jnp.sum(probs, axis=-1, keepdims=True)
            acc = acc * shrink + dot(probs.astype(BF), block[:, HEAD_SIZE:])
            return top, total, acc

        high, total, acc = lax.fori_loop(
            0,
            (segment + 1) * groups,
            step,
            (
                jnp.full((q.shape[0], 1), MASKED, F32),
                jnp.zeros((q.shape[0], 1), F32),
                jnp.zeros((q.shape[0], HEAD_SIZE), F32),
            ),
        )
        unstack_heads(out_ref, segment, acc / total)
        lse_ref[segment] = high + jnp.log(total)


def attend_back_kernel(
    scale, q_ref, kv_ref, qpos_ref, kpos_ref, out_ref, lse_ref, grad_ref, dq_ref, dkv_ref
):
    groups, _, segments, half, wide = kv_ref.shape
    rows = 2 * half
    dkv_ref[...] = jnp.zeros_like(dkv_ref)
    for segment in range(segments):
        q = stack_heads(q_ref, segment)
        grad = stack_heads(grad_ref, segment)
        out = stack_heads(out_ref, segment)
        delta = jnp.sum(out * grad.astype(F32), axis=-1, keepdims=True)
        lse = lse_ref[segment]
        qpos = qpos_ref[segment]
        qpos = jnp.concatenate([qpos] * (q.shape[0] // rows), axis=0)

        def step(index, dq, q=q, grad=grad, delta=delta, lse=lse, qpos=qpos):
            part = lax.div(index, groups)
            group = lax.rem(index, groups)
            block = kv_ref[group, :, part].reshape(rows, wide)
            keys = block[:, :HEAD_SIZE]
            scores = dot_nt(q, keys) * scale
            scores = jnp.where(kpos_ref[index] <= qpos, scores, MASKED)
            probs = jnp.exp(scores - lse)
            d_probs = dot_nt(grad, block[:, HEAD_SIZE:])
            d_scores = (probs * (d_probs - delta)).astype(BF)
            d_keys = dot_tn(d_scores, q) * scale
            d_values = dot_tn(probs.astype(BF), grad)
            both = jnp.concatenate([d_keys, d_values], axis=1).reshape(2, half, wide)
            dkv_ref[group, :, part] = dkv_ref[group, :, part] + both
            return dq + dot(d_scores, keys)

        dq = lax.fori_loop(
            0, (segment + 1) * groups, step, jnp.zeros((q.shape[0], HEAD_SIZE), F32)
        )
        unstack_heads(dq_ref, segment, dq * scale)


def attend(q, kv, qpos, kpos):
    half, wide = q.shape[2], q.shape[3]
    scores = 4 * half * 3 * kv.shape[0] * 2 * half
    return pl.pallas_call(
        functools.partial(attend_kernel, HEAD_SIZE**-0.5),
        out_shape=[
            jax.ShapeDtypeStruct(q.shape, F32),
            jax.ShapeDtypeStruct((q.shape[1], 2 * half * (wide // HEAD_SIZE), 1), F32),
        ],
        compiler_params=pltpu.CompilerParams(vmem_limit_bytes=40 << 20),
        cost_estimate=pl.CostEstimate(
            flops=4 * HEAD_SIZE * scores, bytes_accessed=4 << 20, transcendentals=scores
        ),
        name="attend",
    )(q, kv, qpos, kpos)


def attend_back(q, kv, qpos, kpos, out, lse, grad):
    half = q.shape[2]
    scores = 4 * half * 3 * kv.shape[0] * 2 * half
    return pl.pallas_call(
        functools.partial(attend_back_kernel, HEAD_SIZE**-0.5),
        out_shape=[
            jax.ShapeDtypeStruct(q.shape, F32),
            jax.ShapeDtypeStruct(kv.shape, F32),
        ],
        compiler_params=pltpu.CompilerParams(vmem_limit_bytes=48 << 20),
        cost_estimate=pl.CostEstimate(
            flops=10 * HEAD_SIZE * scores, bytes_accessed=6 << 20, transcendentals=scores
        ),
        name="attend_back",
    )(q, kv, qpos, kpos, out, lse, grad)


def local(
    layer_input,
    query_weight,
    key_matrix,
    value_matrix,
    output_weight,
    gate_weight,
    up_weight,
    down_weight,
    attn_gain,
    mlp_gain,
    query_gain,
    key_gain,
    cotangent,
):
    ways = lax.axis_size("dp")
    place = lax.axis_index("dp")
    side = lax.axis_index("tp")
    segments, _, rows, width = layer_input.shape
    piece = width // ways
    row_bits = [1 << k for k in range(ways.bit_length() - 1) if (1 << k) not in (CORE, SPLIT)]
    mixes = [0]
    for bit in row_bits:
        mixes = mixes + [mix | bit for mix in mixes]
    groups = len(mixes)
    chunk = 4 * piece
    quad = [
        [base, base | CORE, base | SPLIT, base | CORE | SPLIT] for base in mixes
    ]

    def swap(value, bit):
        return lax.ppermute(value, "dp", [(i, i ^ bit) for i in range(ways)])

    def swap_tp(value):
        return lax.ppermute(value, "tp", [(0, 1), (1, 0)])

    def bit_set(bit):
        return (place & bit) != 0

    def turn(blocks):
        for bit in row_bits:
            flag = bit_set(bit)
            blocks = [jnp.where(flag, blocks[k ^ bit], blocks[k]) for k in range(ways)]
        return blocks

    def to_local(value):
        blocks = [value[..., k * piece : (k + 1) * piece] for k in range(ways)]
        blocks = turn(blocks)
        return jnp.concatenate([blocks[k] for four in quad for k in four], axis=-1)

    def from_local(value):
        order = [k for four in quad for k in four]
        where = {k: n for n, k in enumerate(order)}
        blocks = [
            value[..., where[k] * piece : (where[k] + 1) * piece] for k in range(ways)
        ]
        return jnp.concatenate(turn(blocks), axis=-1)

    quads = [[base | CORE * (n & 1) | SPLIT * (n >> 1) for n in range(4)] for base in mixes]

    def trade(value):
        return lax.all_to_all(value, "dp", 0, 0, axis_index_groups=quads, tiled=True)

    def spread(value, order):
        held = {0: value}
        for bit in order:
            for mix in list(held):
                held[mix ^ bit] = swap(held[mix], bit)
        return [held[mix] for mix in mixes]

    def reduce_groups(parts, order):
        held = dict(zip(mixes, parts))
        for bit in order:
            sent = {mix: swap(held[mix].astype(BF), bit) for mix in held if mix & bit}
            held = {
                mix: held[mix] + sent[mix ^ bit].astype(F32) for mix in held if not mix & bit
            }
        return held[0]

    near, far = row_bits, row_bits[::-1]

    def split_columns(weight):
        wide = weight.shape[1] // 4
        return weight.reshape(piece, 4, wide).transpose(1, 0, 2)

    def rows_of(weight):
        return weight.reshape(4, weight.shape[0] // 4, piece)

    def fetch_in(value, order):
        value = trade(value)
        value = value.reshape(chunk, value.shape[2])
        return spread(value, order)

    def fetch_out(value, order):
        value = trade(value)
        value = jnp.concatenate([value[n] for n in range(4)], axis=1)
        return spread(value, order)

    q_parts = fetch_in(split_columns(query_weight), near)
    kv_parts = fetch_in(
        jnp.concatenate([split_columns(key_matrix), split_columns(value_matrix)], axis=2), far
    )
    o_parts = fetch_out(rows_of(output_weight), far)
    gate_parts = fetch_in(split_columns(gate_weight), near)
    up_parts = fetch_in(split_columns(up_weight), far)
    down_parts = fetch_out(rows_of(down_weight), near)

    def gather_rows(value):
        halves = [[], []]
        for s in range(segments):
            held = [value[s]]
            held = held + [swap(v, SPLIT) for v in held]
            held = held + [swap_tp(v) for v in held]
            halves[0] += held
            halves[1] += [swap(v, CORE) for v in held]
        return jnp.concatenate(halves[0] + halves[1], axis=0)

    def scatter_rows(produce):
        mine = 4 * rows
        sent = produce(1).astype(BF)
        kept = produce(0)
        done = []
        for s in range(segments):
            part = slice(s * mine, (s + 1) * mine)
            low = (kept[part] + swap(sent[part], CORE).astype(F32)).astype(BF)
            low = low[: 2 * rows].astype(F32) + swap_tp(low[2 * rows :]).astype(F32)
            low = low.astype(BF)
            low = low[:rows].astype(F32) + swap(low[rows:], SPLIT).astype(F32)
            done.append(low)
        return jnp.stack(done)

    half = 4 * rows
    all_rows = 2 * segments * half
    side_by = segments * half

    index = jnp.arange(all_rows, dtype=jnp.int32)
    row_in = index % rows
    split_by = (index // rows) % 2
    tp_by = (index // (2 * rows)) % 2
    segment_by = (index // half) % segments
    core_by = index // side_by

    def positions(base):
        block = base ^ (split_by * SPLIT) ^ (core_by * CORE)
        return (segment_by * ways + block) * ROWS_DEV + (side ^ tp_by) * rows + row_in

    query_pos = positions(place)
    cosine_table, sine_table = tables(query_pos, HEAD_SIZE)

    def by_segment(pos):
        return pos.reshape(2, segments, half).transpose(1, 0, 2).reshape(segments, 2 * half)

    qpos = by_segment(query_pos)[:, :, None]
    kpos = jnp.stack([by_segment(positions(place ^ mix)) for mix in mixes], axis=1)
    kpos = kpos.reshape(segments * groups, 1, 2 * half)

    attn_gain_local = to_local(attn_gain[None])
    mlp_gain_local = to_local(mlp_gain[None])
    incoming = to_local(cotangent[:, 0])
    incoming_all = gather_rows(incoming)

    resident = to_local(layer_input[:, 0].astype(F32))
    normed = norm_rows(resident, attn_gain_local).astype(BF)
    normed_all = gather_rows(normed)

    q_full = jnp.concatenate(q_parts, axis=0)
    kv_full = jnp.concatenate(kv_parts, axis=0)
    o_full = jnp.concatenate(o_parts, axis=1)
    gate_full = jnp.concatenate(gate_parts, axis=0)
    up_full = jnp.concatenate(up_parts, axis=0)
    down_full = jnp.concatenate(down_parts, axis=1)

    heads_q = q_full.shape[1] // HEAD_SIZE
    q_raw = dot(normed_all, q_full)
    kv_raw = dot(normed_all, kv_full)
    key_raw = kv_raw[:, :HEAD_SIZE]
    value_rows = kv_raw[:, HEAD_SIZE:].astype(BF)
    q_raws = [q_raw[:, h * HEAD_SIZE : (h + 1) * HEAD_SIZE] for h in range(heads_q)]

    def prepare(raw_in, gain_in):
        return rotate(norm_rows(raw_in, gain_in), cosine_table, sine_table)

    query_rows = jnp.concatenate([prepare(v, query_gain).astype(BF) for v in q_raws], axis=1)
    key_rows = prepare(key_raw, key_gain).astype(BF)
    keys_all = spread(key_rows, near)
    values_all = spread(value_rows, far)
    kv_all = jnp.stack(
        [jnp.concatenate([k, v], axis=1) for k, v in zip(keys_all, values_all)]
    ).reshape(groups, 2, segments, half, 2 * HEAD_SIZE)
    q4 = query_rows.reshape(2, segments, half, heads_q * HEAD_SIZE)
    attended, lse = attend(q4, kv_all, qpos, kpos)
    heads = attended.astype(BF).reshape(all_rows, heads_q * HEAD_SIZE)

    def of_side(value, c):
        return value[c * side_by : (c + 1) * side_by]

    branch = scatter_rows(lambda c: dot(of_side(heads, c), o_full))
    middle = resident + branch
    normed2 = norm_rows(middle, mlp_gain_local).astype(BF)
    normed2_all = gather_rows(normed2)
    gate_pre = dot(normed2_all, gate_full)
    up_pre = dot(normed2_all, up_full)
    active = (jax.nn.silu(gate_pre) * up_pre).astype(BF)
    mlp_out = scatter_rows(lambda c: dot(of_side(active, c), down_full))
    layer_output = from_local((middle + mlp_out).astype(BF))[:, None]

    d_active = dot_nt(incoming_all, down_full)
    sigma = jax.nn.sigmoid(gate_pre)
    d_gate = (d_active * up_pre * sigma * (1.0 + gate_pre * (1.0 - sigma))).astype(BF)
    d_upper = (d_active * gate_pre * sigma).astype(BF)
    d_normed2 = scatter_rows(
        lambda c: dot_nt(of_side(d_gate, c), gate_full) + dot_nt(of_side(d_upper, c), up_full)
    )

    def part_of(value, j):
        return value[:, j * chunk : (j + 1) * chunk]

    def grad_in(rows_in, grad_rows, order):
        parts = [dot_tn(part_of(rows_in, j), grad_rows) for j in range(groups)]
        total = reduce_groups(parts, order).astype(BF)
        return trade(total.reshape(4, piece, total.shape[1])).astype(F32)

    def grad_out(rows_in, grad_rows, order):
        parts = [dot_tn(rows_in, part_of(grad_rows, j)) for j in range(groups)]
        total = reduce_groups(parts, order).astype(BF)
        total = jnp.stack([total[:, n * piece : (n + 1) * piece] for n in range(4)])
        return trade(total).astype(F32)

    def join_columns(value):
        return jnp.concatenate([value[n] for n in range(4)], axis=1)

    def join_rows(value):
        return value.reshape(4 * value.shape[1], piece)

    down_grad = join_rows(grad_out(active, incoming_all, far))
    gate_grad = join_columns(grad_in(normed2_all, d_gate, far))
    up_grad = join_columns(grad_in(normed2_all, d_upper, near))

    _, pull_mlp = jax.vjp(norm_rows, middle, mlp_gain_local)
    d_mid_norm, d_mlp_gain = pull_mlp(d_normed2)
    d_middle = incoming.astype(F32) + d_mid_norm
    d_branch_all = gather_rows(d_middle.astype(BF))
    d_heads = dot_nt(d_branch_all, o_full).astype(BF)
    output_grad = join_rows(grad_out(heads, d_branch_all, near))

    dq, dkv = attend_back(
        q4, kv_all, qpos, kpos, attended, lse, d_heads.reshape(q4.shape)
    )
    dkv = dkv.reshape(groups, all_rows, 2 * HEAD_SIZE)
    d_keys = reduce_groups([dkv[j, :, :HEAD_SIZE] for j in range(groups)], far)
    d_values = reduce_groups([dkv[j, :, HEAD_SIZE:] for j in range(groups)], near)
    dq = dq.reshape(all_rows, heads_q * HEAD_SIZE)

    d_q_raws = []
    d_query_gain = jnp.zeros_like(query_gain)
    for h in range(heads_q):
        _, pull_query = jax.vjp(prepare, q_raws[h], query_gain)
        d_raw, d_gain = pull_query(dq[:, h * HEAD_SIZE : (h + 1) * HEAD_SIZE])
        d_q_raws.append(d_raw.astype(BF))
        d_query_gain = d_query_gain + d_gain
    d_q_low = jnp.concatenate(d_q_raws, axis=1)
    _, pull_key = jax.vjp(prepare, key_raw, key_gain)
    d_k_raw, d_key_gain = pull_key(d_keys)
    d_kv_low = jnp.concatenate([d_k_raw.astype(BF), d_values.astype(BF)], axis=1)

    d_normed = scatter_rows(
        lambda c: dot_nt(of_side(d_q_low, c), q_full) + dot_nt(of_side(d_kv_low, c), kv_full)
    )
    query_grad = join_columns(grad_in(normed_all, d_q_low, far))
    kv_grad = grad_in(normed_all, d_kv_low, near)
    key_grad = join_columns(kv_grad[:, :, :HEAD_SIZE])
    value_grad = join_columns(kv_grad[:, :, HEAD_SIZE:])

    _, pull_attn = jax.vjp(norm_rows, resident, attn_gain_local)
    d_resident, d_attn_gain = pull_attn(d_normed)
    input_grad = from_local((d_middle + d_resident).astype(BF))[:, None]

    gains = jnp.concatenate(
        [
            from_local(d_attn_gain)[0],
            from_local(d_mlp_gain)[0],
            d_query_gain,
            d_key_gain,
        ]
    ).reshape(-1, 128)
    for bit in [CORE, SPLIT] + row_bits:
        gains = gains + swap(gains, bit)
    gains = (gains + swap_tp(gains)).reshape(-1)
    gain_attn = gains[:width]
    gain_mlp = gains[width : 2 * width]
    gain_query = gains[2 * width : 2 * width + HEAD_SIZE]
    gain_key = gains[2 * width + HEAD_SIZE :]
    return (
        layer_output,
        input_grad,
        query_grad,
        key_grad,
        value_grad,
        output_grad,
        gate_grad,
        up_grad,
        down_grad,
        gain_attn,
        gain_mlp,
        gain_query,
        gain_key,
    )


def solution(mesh):
    in_specs = (
        P(None, "dp", "tp", None),
        P("dp", "tp"),
        P("dp", "tp"),
        P("dp", "tp"),
        P("tp", "dp"),
        P("dp", "tp"),
        P("dp", "tp"),
        P("tp", "dp"),
        P(),
        P(),
        P(),
        P(),
        P(None, "dp", "tp", None),
    )
    out_specs = (
        P(None, "dp", "tp", None),
        P(None, "dp", "tp", None),
        P("dp", "tp"),
        P("dp", "tp"),
        P("dp", "tp"),
        P("tp", "dp"),
        P("dp", "tp"),
        P("dp", "tp"),
        P("tp", "dp"),
        P(),
        P(),
        P(),
        P(),
    )
    return jax.shard_map(local, mesh=mesh, in_specs=in_specs, out_specs=out_specs, check_vma=False)
```

```python
import functools

import jax
import jax.numpy as jnp
from jax import lax
from jax.experimental import pallas as pl
from jax.experimental.pallas import tpu as pltpu
from jax.sharding import PartitionSpec as P

HEAD_SIZE = 128
ROWS_DEV = 64

EPSILON = 1e-06
ROPE_BASE = 1000000.0
MASKED = -1e30

CORE = 1
SPLIT = 8

BF = jnp.bfloat16
F32 = jnp.float32
MIB = 1 << 20


def dot(left, right):
    return jnp.dot(left, right, preferred_element_type=F32)


def dot_nt(left, right):
    return lax.dot_general(left, right, (((1,), (1,)), ((), ())), preferred_element_type=F32)


def dot_tn(left, right):
    return lax.dot_general(left, right, (((0,), (0,)), ((), ())), preferred_element_type=F32)


def tables(positions, head_width):
    half_width = head_width // 2
    inverse = ROPE_BASE ** (-(jnp.arange(half_width, dtype=F32) * 2.0 / head_width))
    angles = positions.astype(F32)[:, None] * inverse[None, :]
    angles = jnp.concatenate([angles, angles], axis=-1)
    return (jnp.cos(angles), jnp.sin(angles))


def call(body, name, outs, ins, ties=(), scratch=(), limit=32, specs=None):
    ins, ties = list(ins), list(ties)
    count = len(ins)

    def kernel(*refs):
        body(*refs[:count], *refs[count + len(ties) :])

    in_specs = [pl.BlockSpec(memory_space=pltpu.VMEM)] * count
    for at, spec in (specs or {}).items():
        in_specs[at] = spec
    return pl.pallas_call(
        kernel,
        grid=(1,) if specs else (),
        out_shape=[jax.ShapeDtypeStruct(s, d) for s, d in outs],
        in_specs=in_specs + [pl.BlockSpec(memory_space=pl.ANY)] * len(ties),
        out_specs=[pl.BlockSpec(memory_space=pltpu.VMEM)] * len(outs),
        scratch_shapes=list(scratch),
        compiler_params=pltpu.CompilerParams(vmem_limit_bytes=limit * MIB),
        cost_estimate=pl.CostEstimate(flops=0, bytes_accessed=0, transcendentals=0),
        name=name,
    )(*ins, *ties)


def rms(value):
    return lax.rsqrt(jnp.mean(value * value, axis=-1, keepdims=True) + EPSILON)


def flip_sign(shape):
    lane = lax.broadcasted_iota(jnp.int32, shape, 1)
    return jnp.where(lane < HEAD_SIZE // 2, -1.0, 1.0).astype(F32)


def rope(raw, gain, cosine, sine):
    scaled = raw * rms(raw) * gain
    turned = pltpu.roll(scaled, HEAD_SIZE // 2, 1) * flip_sign(scaled.shape)
    return scaled * cosine + turned * sine


def rope_back(grad, raw, gain, cosine, sine):
    swung = grad * sine
    turned = pltpu.roll(swung, HEAD_SIZE // 2, 1) * flip_sign(swung.shape)
    d_scaled = grad * cosine - turned
    scale = rms(raw)
    unit = raw * scale
    d_gain = jnp.sum(d_scaled * unit, axis=0, keepdims=True)
    d_unit = d_scaled * gain
    d_raw = scale * (d_unit - unit * jnp.mean(d_unit * unit, axis=-1, keepdims=True))
    return d_raw, d_gain


def norm_back(grad, value, gain):
    scale = rms(value)
    unit = value * scale
    d_gain = jnp.sum(grad * unit, axis=0, keepdims=True)
    d_unit = grad * gain
    return scale * (d_unit - unit * jnp.mean(d_unit * unit, axis=-1, keepdims=True)), d_gain


def assemble(pieces, out_ref, segments, rows):
    block = len(pieces) * rows
    for m, piece in enumerate(pieces):
        for s in range(segments):
            out_ref[s * block + m * rows : s * block + (m + 1) * rows, :] = piece[
                s * rows : (s + 1) * rows, :
            ]


def local(
    layer_input,
    query_weight,
    key_matrix,
    value_matrix,
    output_weight,
    gate_weight,
    up_weight,
    down_weight,
    attn_gain,
    mlp_gain,
    query_gain,
    key_gain,
    cotangent,
):
    ways = lax.axis_size("dp")
    place = lax.axis_index("dp")
    side = lax.axis_index("tp")
    segments, _, rows, width = layer_input.shape
    piece = width // ways
    row_bits = [1 << k for k in range(ways.bit_length() - 1) if (1 << k) not in (CORE, SPLIT)]
    near, far = row_bits, row_bits[::-1]
    groups = 1 << len(row_bits)
    chunk = 4 * piece
    block = 8 * rows
    half = 4 * rows
    all_rows = segments * block
    own = segments * rows
    scale = HEAD_SIZE**-0.5
    wide_q = query_weight.shape[1] // 4
    heads_q = wide_q // HEAD_SIZE
    wide_f = gate_weight.shape[1] // 4

    def mix_list(order):
        mixes = [0]
        for bit in reversed(order):
            mixes = mixes + [mix | bit for mix in mixes]
        return mixes

    mixes = mix_list(near)
    slot = {mix: j for j, mix in enumerate(mixes)}
    quads = [[mix | CORE * (n & 1) | SPLIT * (n >> 1) for n in range(4)] for mix in mixes]
    local_order = [k for four in quads for k in four]

    def swap(value, bit):
        with jax.named_scope("swap%d" % bit):
            return lax.ppermute(value, "dp", [(i, i ^ bit) for i in range(ways)])

    def swap_tp(value):
        with jax.named_scope("swaptp"):
            return lax.ppermute(value, "tp", [(0, 1), (1, 0)])

    def trade(value, name):
        with jax.named_scope(name):
            return lax.all_to_all(value, "dp", 0, 0, axis_index_groups=quads, tiled=True)

    def turn(blocks):
        for bit in row_bits:
            flag = (place & bit) != 0
            blocks = [jnp.where(flag, blocks[k ^ bit], blocks[k]) for k in range(ways)]
        return blocks

    def to_local(value):
        blocks = turn([value[..., k * piece : (k + 1) * piece] for k in range(ways)])
        return jnp.concatenate([blocks[k] for k in local_order], axis=-1)

    def from_local(value):
        where = {k: n for n, k in enumerate(local_order)}
        blocks = [value[..., where[k] * piece : (where[k] + 1) * piece] for k in range(ways)]
        return jnp.concatenate(turn(blocks), axis=-1)

    def spread(value, order, name):
        held = {0: value}
        with jax.named_scope(name):
            for bit in order:
                for mix in list(held):
                    held[mix ^ bit] = swap(held[mix], bit)
        return [held[mix] for mix in mixes]

    wide_k = 2 * HEAD_SIZE
    wide_1 = 2 * wide_q + wide_k

    def pack_first(q_ref, k_ref, v_ref, o_ref, out_ref):
        for n in range(4):
            out_ref[n, :, :wide_q] = q_ref[:, n * wide_q : (n + 1) * wide_q]
            for at, ref in ((wide_q, k_ref), (wide_q + HEAD_SIZE, v_ref)):
                out_ref[n, :, at : at + HEAD_SIZE] = ref[:, n * HEAD_SIZE : (n + 1) * HEAD_SIZE]
            for b in range(0, wide_q, piece):
                at = wide_q + wide_k + b
                out_ref[n, :, at : at + piece] = o_ref[n * wide_q + b : n * wide_q + b + piece, :]

    def pack_columns(ref, out_ref):
        for n in range(4):
            out_ref[n] = ref[:, n * wide_f : (n + 1) * wide_f]

    (packed,) = call(
        pack_first,
        "pack1",
        [((4, piece, wide_1), BF)],
        [query_weight, key_matrix, value_matrix, output_weight],
    )
    wide_shape = ((4, piece, wide_f), BF)
    first = trade(packed, "t_first").reshape(chunk, wide_1)
    (packed,) = call(pack_columns, "pack2", [wide_shape], [gate_weight])
    gate = trade(packed, "t_gate").reshape(chunk, wide_f)
    (packed,) = call(pack_columns, "pack3", [wide_shape], [up_weight], ties=[gate])
    up = trade(packed, "t_up").reshape(chunk, wide_f)
    down = trade(down_weight.reshape(4, wide_f, piece), "t_down")
    q_parts = spread(first[:, :wide_q], near, "s_q")
    kv_parts = spread(first[:, wide_q : wide_q + wide_k], far, "s_kv")
    o_parts = spread(first[:, wide_q + wide_k :], near, "s_o")
    gate_parts = spread(gate, near, "s_gate")
    up_parts = spread(up, far, "s_up")
    down_parts = spread(down, near, "s_down")

    def gather_rows(value, name):
        held = [value]
        with jax.named_scope(name):
            held = held + [swap(v, SPLIT) for v in held]
            held = held + [swap_tp(v) for v in held]
            return held + [swap(v, CORE) for v in held]

    def add_split(kept, got, name, ties=()):
        count = kept.shape[1] // 2

        def body(kept_ref, got_ref, sent_out, kept_out):
            total = kept_ref[...].astype(F32) + got_ref[...].astype(F32)
            kept_out[...] = total[:, :count].astype(BF)
            sent_out[...] = total[:, count:].astype(BF)

        shape = (segments, count, width)
        return call(body, name, [(shape, BF), (shape, BF)], [kept, got], ties=ties)

    def scatter_rows(sent, kept, name, ties_c=(), ties_t=()):
        with jax.named_scope(name):
            sent, kept = add_split(kept, swap(sent, CORE), name + "_c", ties_c)
            sent, kept = add_split(kept, swap_tp(sent), name + "_t", ties_t)
            return kept.reshape(own, width), swap(sent, SPLIT).reshape(own, width)

    pair = [((segments, half, width), BF)] * 2

    def store_pair(sent_ref, kept_ref, s, value, at):
        stop = at + value.shape[1]
        kept_ref[s, :, at:stop] = value[:half].astype(BF)
        sent_ref[s, :, at:stop] = value[half:].astype(BF)

    index = jnp.arange(all_rows, dtype=jnp.int32)
    segment_by = index // block
    m_by = (index // rows) % 8

    def positions(base):
        at = base ^ ((m_by & 1) * SPLIT) ^ ((m_by >> 2) * CORE)
        return (
            (segment_by * ways + at) * ROWS_DEV
            + (side ^ ((m_by >> 1) & 1)) * rows
            + index % rows
        )

    query_pos = positions(place)
    cosine, sine = tables(query_pos, HEAD_SIZE)
    qpos = query_pos[:, None]
    kpos = jnp.stack([positions(place ^ mix).reshape(segments, block) for mix in mixes], axis=1)
    kpos = kpos.reshape(1, segments * groups * block)
    span = min(groups, 2)

    gain_q, gain_k = query_gain[None], key_gain[None]
    row_mask = ways - 1 - CORE - SPLIT
    where_spec = pl.BlockSpec(memory_space=pltpu.SMEM)
    where = (place & row_mask)[None]

    def lanes_of(where_ref, n):
        return pl.ds(pl.multiple_of((local_order[n] ^ where_ref[0]) * piece, piece), piece)

    def enter(where_ref, x_ref, c_ref, ga_ref, gm_ref, x_out, c_out, ga_out, gm_out, out_ref):
        for n in range(ways):
            lanes, here = lanes_of(where_ref, n), slice(n * piece, (n + 1) * piece)
            x_out[:, here] = x_ref[:, lanes]
            c_out[:, here] = c_ref[:, lanes]
            ga_out[:, here] = ga_ref[:, lanes]
            gm_out[:, here] = gm_ref[:, lanes]
        value = x_out[...].astype(F32)
        out_ref[...] = (value * rms(value) * ga_out[...]).astype(BF)

    own_shape, line_shape = (own, width), (1, width)
    if piece % 128 == 0:
        x_own, c_own, gain_a, gain_m, normed = call(
            enter,
            "enter",
            [
                (own_shape, BF),
                (own_shape, BF),
                (line_shape, F32),
                (line_shape, F32),
                (own_shape, BF),
            ],
            [
                where,
                layer_input.reshape(own_shape),
                cotangent.reshape(own_shape),
                attn_gain[None],
                mlp_gain[None],
            ],
            specs={0: where_spec},
        )
    else:
        x_own = to_local(layer_input.reshape(own_shape))
        c_own = to_local(cotangent.reshape(own_shape))
        gain_a = to_local(attn_gain[None])
        gain_m = to_local(mlp_gain[None])

        def first_norm(x_ref, gain_ref, out_ref):
            value = x_ref[...].astype(F32)
            out_ref[...] = (value * rms(value) * gain_ref[...]).astype(BF)

        (normed,) = call(first_norm, "norm1", [(own_shape, BF)], [x_own, gain_a])

    def put_back(values, name):
        if piece % 128:
            return [from_local(v) for v in values]

        def body(*refs):
            where_ref, ins, outs = refs[0], refs[1 : 1 + len(values)], refs[1 + len(values) :]
            for in_ref, out_ref in zip(ins, outs):
                for n in range(ways):
                    out_ref[:, lanes_of(where_ref, n)] = in_ref[:, n * piece : (n + 1) * piece]

        outs = [(v.shape, v.dtype) for v in values]
        return call(body, name, outs, [where, *values], specs={0: where_spec})

    normed_parts = gather_rows(normed, "g_norm1")
    c_parts = gather_rows(c_own, "g_cot")

    def project(*refs):
        parts, refs = refs[:8], refs[8:]
        wq, wkv, refs = refs[:groups], refs[groups : 2 * groups], refs[2 * groups :]
        cos_ref, sin_ref, gq_ref, gk_ref, x_ref, q_ref, kv_ref, q_raw_ref, k_raw_ref = refs
        assemble(parts, x_ref, segments, rows)
        for s in range(segments):
            at = slice(s * block, (s + 1) * block)
            q = sum(dot(x_ref[at, j * chunk : (j + 1) * chunk], wq[j][...]) for j in range(groups))
            kv = sum(
                dot(x_ref[at, j * chunk : (j + 1) * chunk], wkv[j][...]) for j in range(groups)
            )
            q_raw_ref[at, :] = q
            k_raw_ref[at, :] = kv[:, :HEAD_SIZE]
            cos, sin = cos_ref[at, :], sin_ref[at, :]
            for h in range(heads_q):
                lanes = slice(h * HEAD_SIZE, (h + 1) * HEAD_SIZE)
                q_ref[at, lanes] = rope(q[:, lanes], gq_ref[...], cos, sin).astype(BF)
            kv_ref[at, :HEAD_SIZE] = rope(kv[:, :HEAD_SIZE], gk_ref[...], cos, sin).astype(BF)
            kv_ref[at, HEAD_SIZE:] = kv[:, HEAD_SIZE:].astype(BF)

    normed_all, q, kv, q_raw, k_raw = call(
        project,
        "project",
        [
            ((all_rows, width), BF),
            ((all_rows, wide_q), BF),
            ((all_rows, 2 * HEAD_SIZE), BF),
            ((all_rows, wide_q), F32),
            ((all_rows, HEAD_SIZE), F32),
        ],
        [*normed_parts, *q_parts, *kv_parts, cosine, sine, gain_q, gain_k],
        ties=[gate],
    )
    kv_all = spread(kv, near, "s_keys")

    def load_keys(parts, scratch):
        for j, part in enumerate(parts):
            for s in range(segments):
                scratch[s * groups + j] = part[s * block : (s + 1) * block, :]

    def stack_heads(ref, s):
        at = slice(s * block, (s + 1) * block)
        return jnp.concatenate(
            [ref[at, h * HEAD_SIZE : (h + 1) * HEAD_SIZE] for h in range(heads_q)], axis=0
        )

    def load_out_weight(parts, scratch):
        for j, part in enumerate(parts):
            for n in range(4):
                at = (4 * j + n) * piece
                for b in range(0, wide_q, piece):
                    scratch[b : b + piece, at : at + piece] = part[
                        n * piece : (n + 1) * piece, b : b + piece
                    ]

    def load_down_weight(parts, scratch):
        for j, part in enumerate(parts):
            for n in range(4):
                at = (4 * j + n) * piece
                scratch[:, at : at + piece] = part[n]

    strip = min(chunk * groups, 512)

    def attend(*refs):
        kv_refs, wo, refs = refs[:groups], refs[groups : 2 * groups], refs[2 * groups :]
        q_ref, qpos_ref, kpos_ref, out_ref, lse_ref, sent_ref, kept_ref, keys, w_out = refs
        load_keys(kv_refs, keys)
        load_out_weight(wo, w_out)
        for s in range(segments):
            at = slice(s * block, (s + 1) * block)
            q = stack_heads(q_ref, s)
            pos = jnp.concatenate([qpos_ref[at, :]] * heads_q, axis=0)

            high = jnp.full((q.shape[0], 1), MASKED, F32)
            summed = jnp.zeros((q.shape[0], 1), F32)
            acc = jnp.zeros((q.shape[0], HEAD_SIZE), F32)
            for n in range(0, (s + 1) * groups, span):
                both = keys[n : n + span].reshape(span * block, 2 * HEAD_SIZE)
                scores = dot_nt(q, both[:, :HEAD_SIZE]) * scale
                key_at = kpos_ref[:, n * block : (n + span) * block]
                scores = jnp.where(key_at <= pos, scores, MASKED)
                top = jnp.maximum(high, jnp.max(scores, axis=-1, keepdims=True))
                shrink = jnp.exp(high - top)
                probs = jnp.exp(scores - top)
                summed = summed * shrink + jnp.sum(probs, axis=-1, keepdims=True)
                acc = acc * shrink + dot(probs.astype(BF), both[:, HEAD_SIZE:])
                high = top
            acc = acc / summed
            lse_ref[s] = high + jnp.log(summed)
            acc = jnp.concatenate(
                [acc[h * block : (h + 1) * block] for h in range(heads_q)], axis=1
            )
            out_ref[at, :] = acc
            heads = acc.astype(BF)
            for n in range(0, width, strip):
                store_pair(sent_ref, kept_ref, s, dot(heads, w_out[:, n : n + strip]), n)

    attended, lse, sent, kept = call(
        attend,
        "attend",
        [
            ((all_rows, wide_q), F32),
            ((segments, heads_q * block, 1), F32),
            *pair,
        ],
        [*kv_all, *o_parts, q, qpos, kpos],
        ties=[up],
        scratch=[
            pltpu.VMEM((segments * groups, block, 2 * HEAD_SIZE), BF),
            pltpu.VMEM((wide_q, width), BF),
        ],
        limit=40,
    )
    kept, got = scatter_rows(
        sent, kept, "rs1", [gate_parts[slot[near[0]]]], [down, c_parts[1], gate_parts[slot[far[0]]]]
    )

    def second_norm(x_ref, kept_ref, got_ref, gain_ref, mid_ref, out_ref):
        value = x_ref[...].astype(F32) + (
            kept_ref[...].astype(F32) + got_ref[...].astype(F32)
        )
        mid_ref[...] = value
        out_ref[...] = (value * rms(value) * gain_ref[...]).astype(BF)

    middle, normed2 = call(
        second_norm,
        "norm2",
        [((own, width), F32), ((own, width), BF)],
        [x_own, kept, got, gain_m],
        ties=[*c_parts, *gate_parts, up_parts[slot[far[0]]]],
    )
    normed2_parts = gather_rows(normed2, "g_norm2")

    def feed(*refs):
        parts, c_refs, refs = refs[:8], refs[8:16], refs[16:]
        wg, wu, wd = refs[:groups], refs[groups : 2 * groups], refs[2 * groups : 3 * groups]
        (
            x_ref,
            c_ref,
            active_ref,
            dg_ref,
            du_ref,
            sent_ref,
            kept_ref,
            w_down,
        ) = refs[3 * groups :]
        assemble(parts, x_ref, segments, rows)
        assemble(c_refs, c_ref, segments, rows)
        load_down_weight(wd, w_down)

        for s in range(segments):
            at = slice(s * block, (s + 1) * block)
            gate_pre = sum(
                dot(x_ref[at, j * chunk : (j + 1) * chunk], wg[j][...]) for j in range(groups)
            )
            up_pre = sum(
                dot(x_ref[at, j * chunk : (j + 1) * chunk], wu[j][...]) for j in range(groups)
            )
            sigma = jax.nn.sigmoid(gate_pre)
            swish = gate_pre * sigma
            active_ref[at, :] = (swish * up_pre).astype(BF)
            d_active = dot_nt(c_ref[at, :], w_down[...])
            d_gate = (d_active * up_pre * sigma * (1.0 + gate_pre * (1.0 - sigma))).astype(BF)
            d_upper = (d_active * swish).astype(BF)
            dg_ref[at, :] = d_gate
            du_ref[at, :] = d_upper
            for j in range(groups):
                value = dot_nt(d_gate, wg[j][...]) + dot_nt(d_upper, wu[j][...])
                lanes = slice(j * chunk, (j + 1) * chunk)
                kept_ref[s, :, lanes] = value[:half].astype(BF)
                sent_ref[s, :, lanes] = value[half:].astype(BF)

    normed2_all, c_all, active, d_gate, d_upper, sent, kept = call(
        feed,
        "feed",
        [
            ((all_rows, width), BF),
            ((all_rows, width), BF),
            ((all_rows, wide_f), BF),
            ((all_rows, wide_f), BF),
            ((all_rows, wide_f), BF),
            *pair,
        ],
        [*normed2_parts, *c_parts, *gate_parts, *up_parts, *down_parts],
        scratch=[pltpu.VMEM((wide_f, width), BF)],
        limit=52,
    )
    kept, got = scatter_rows(sent, kept, "rs2")

    def grad_in(x_all, grads, orders, name):
        lists = [mix_list(order) for order in orders]

        def body(*refs):
            x_ref, g_refs, outs = refs[0], refs[1 : 1 + len(grads)], refs[1 + len(grads) :]
            for g_ref, mix, n in zip(g_refs, lists, range(len(grads))):
                for at, which in enumerate(mix):
                    j = slot[which]
                    value = dot_tn(x_ref[:, j * chunk : (j + 1) * chunk], g_ref[...]).astype(BF)
                    if at < groups // 2:
                        outs[2 * n + 1][at] = value
                    else:
                        outs[2 * n][at - groups // 2] = value

        outs = []
        for g in grads:
            outs += [((groups // 2, chunk, g.shape[1]), BF)] * 2
        return call(body, name, outs, [x_all, *grads], limit=48)

    def grad_out(left, c_value, order, name):
        mix = mix_list(order)
        tall = left.shape[1]

        def body(left_ref, c_ref, sent_ref, kept_ref):
            for at, which in enumerate(mix):
                j = slot[which]
                value = dot_tn(
                    left_ref[...].astype(BF), c_ref[:, j * chunk : (j + 1) * chunk]
                ).astype(BF)
                for n in range(4):
                    part = value[:, n * piece : (n + 1) * piece]
                    if at < groups // 2:
                        kept_ref[at, n] = part
                    else:
                        sent_ref[at - groups // 2, n] = part

        return call(
            body, name, [((groups // 2, 4, tall, piece), BF)] * 2, [left, c_value], limit=48
        )

    def reduce_groups(sent, kept, order, name):
        with jax.named_scope(name):
            for bit in order[:-1]:
                total = kept.astype(F32) + swap(sent, bit).astype(F32)
                count = total.shape[0] // 2
                kept, sent = total[:count].astype(BF), total[count:].astype(BF)
            return (kept.astype(F32) + swap(sent, order[-1]).astype(F32))[0]

    down_sums = reduce_groups(*grad_out(active, c_all, near, "w_down"), near, "r_down")
    gate_sent, gate_kept, up_sent, up_kept = grad_in(
        normed2_all, [d_gate, d_upper], [near, far], "w_gate_up"
    )
    gate_sums = reduce_groups(gate_sent, gate_kept, near, "r_gate")
    up_sums = reduce_groups(up_sent, up_kept, far, "r_up")
    down_grad = trade(down_sums.astype(BF), "t_ddown").astype(F32).reshape(4 * wide_f, piece)
    gate_up = jnp.concatenate([gate_sums, up_sums], axis=1).astype(BF)
    gate_up = trade(gate_up.reshape(4, piece, 2 * wide_f), "t_dgu").astype(F32)

    def join(value, start, stop):
        return jnp.concatenate([value[n, :, start:stop] for n in range(4)], axis=1)

    gate_grad = join(gate_up, 0, wide_f)
    up_grad = join(gate_up, wide_f, 2 * wide_f)

    def norm_step_back(kept_ref, got_ref, mid_ref, gain_ref, c_ref, d_ref, low_ref, gain_out):
        grad = kept_ref[...].astype(F32) + got_ref[...].astype(F32)
        back, gain_grad = norm_back(grad, mid_ref[...], gain_ref[...])
        total = c_ref[...].astype(F32) + back
        d_ref[...] = total
        low_ref[...] = total.astype(BF)
        gain_out[...] = gain_grad

    d_middle, d_branch, d_gain_m = call(
        norm_step_back,
        "norm2_back",
        [((own, width), F32), ((own, width), BF), ((1, width), F32)],
        [kept, got, middle, gain_m, c_own],
    )
    d_parts = gather_rows(d_branch, "g_branch")

    def feed_out(*refs):
        wd, refs = refs[:groups], refs[groups:]
        active_ref, sent_ref, kept_ref, w_down = refs
        load_down_weight(wd, w_down)
        for s in range(segments):
            at = slice(s * block, (s + 1) * block)
            for n in range(0, width, strip):
                store_pair(
                    sent_ref, kept_ref, s, dot(active_ref[at, :], w_down[:, n : n + strip]), n
                )

    out_sent, out_kept = call(
        feed_out,
        "feed_out",
        pair,
        [*down_parts, active],
        ties=[],
        scratch=[pltpu.VMEM((wide_f, width), BF)],
    )
    out_kept, out_got = scatter_rows(out_sent, out_kept, "rs3")
    layer_output = (middle + (out_kept.astype(F32) + out_got.astype(F32))).astype(BF)
    layer_output = put_back([layer_output], "leave1")[0].reshape(layer_input.shape)

    key_mix, value_mix = mix_list(near), mix_list(far)

    def attend_back(*refs):
        parts, kv_refs, wo = refs[:8], refs[8 : 8 + groups], refs[8 + groups : 8 + 2 * groups]
        (
            q_ref,
            qpos_ref,
            kpos_ref,
            out_ref,
            lse_ref,
            q_raw_ref,
            cos_ref,
            sin_ref,
            gq_ref,
            d_all_ref,
            dq_ref,
            gain_out,
            k_sent,
            k_kept,
            v_sent,
            v_kept,
            keys,
            w_out,
            sums,
        ) = refs[8 + 2 * groups :]
        assemble(parts, d_all_ref, segments, rows)
        load_keys(kv_refs, keys)
        load_out_weight(wo, w_out)
        sums[...] = jnp.zeros_like(sums)
        gain_total = jnp.zeros((1, HEAD_SIZE), F32)
        for s in range(segments):
            at = slice(s * block, (s + 1) * block)
            q = stack_heads(q_ref, s)
            out = stack_heads(out_ref, s)
            d_heads = dot_nt(d_all_ref[at, :], w_out[...]).astype(BF)
            grad = jnp.concatenate(
                [d_heads[:, h * HEAD_SIZE : (h + 1) * HEAD_SIZE] for h in range(heads_q)], axis=0
            )
            delta = jnp.sum(out * grad.astype(F32), axis=-1, keepdims=True)
            lse = lse_ref[s]
            pos = jnp.concatenate([qpos_ref[at, :]] * heads_q, axis=0)

            dq = jnp.zeros((q.shape[0], HEAD_SIZE), F32)
            for n in range(0, (s + 1) * groups, span):
                both = keys[n : n + span].reshape(span * block, 2 * HEAD_SIZE)
                key = both[:, :HEAD_SIZE]
                scores = dot_nt(q, key) * scale
                key_at = kpos_ref[:, n * block : (n + span) * block]
                scores = jnp.where(key_at <= pos, scores, MASKED)
                probs = jnp.exp(scores - lse)
                d_probs = dot_nt(grad, both[:, HEAD_SIZE:])
                d_scores = (probs * (d_probs - delta)).astype(BF)
                d_keys = dot_tn(d_scores, q) * scale
                d_values = dot_tn(probs.astype(BF), grad)
                both = jnp.concatenate([d_keys, d_values], axis=1)
                both = both.reshape(span, block, 2 * HEAD_SIZE)
                sums[n : n + span] = sums[n : n + span] + both
                dq = dq + dot(d_scores, key)
            dq = dq * scale
            for h in range(heads_q):
                lanes = slice(h * HEAD_SIZE, (h + 1) * HEAD_SIZE)
                d_raw, d_gain = rope_back(
                    dq[h * block : (h + 1) * block],
                    q_raw_ref[at, lanes],
                    gq_ref[...],
                    cos_ref[at, :],
                    sin_ref[at, :],
                )
                dq_ref[at, lanes] = d_raw.astype(BF)
                gain_total = gain_total + d_gain
        gain_out[...] = gain_total
        for mix, lane, sent_ref, kept_ref in (
            (key_mix, 0, k_sent, k_kept),
            (value_mix, HEAD_SIZE, v_sent, v_kept),
        ):
            for n, which in enumerate(mix):
                for s in range(segments):
                    value = sums[s * groups + slot[which], :, lane : lane + HEAD_SIZE].astype(BF)
                    rows_at = slice(s * block, (s + 1) * block)
                    if n < groups // 2:
                        kept_ref[n, rows_at, :] = value
                    else:
                        sent_ref[n - groups // 2, rows_at, :] = value

    part_shape = ((groups // 2, all_rows, HEAD_SIZE), BF)
    d_all, d_q, d_gain_q, k_sent, k_kept, v_sent, v_kept = call(
        attend_back,
        "attend_back",
        [
            ((all_rows, width), BF),
            ((all_rows, wide_q), BF),
            ((1, HEAD_SIZE), F32),
            part_shape,
            part_shape,
            part_shape,
            part_shape,
        ],
        [
            *d_parts,
            *kv_all,
            *o_parts,
            q,
            qpos,
            kpos,
            attended,
            lse,
            q_raw,
            cosine,
            sine,
            gain_q,
        ],
        scratch=[
            pltpu.VMEM((segments * groups, block, 2 * HEAD_SIZE), BF),
            pltpu.VMEM((wide_q, width), BF),
            pltpu.VMEM((segments * groups, block, 2 * HEAD_SIZE), F32),
        ],
        limit=52,
    )

    out_sums = reduce_groups(*grad_out(attended, d_all, near, "w_out"), near, "r_out")
    output_grad = trade(out_sums.astype(BF), "t_dout").astype(F32).reshape(4 * wide_q, piece)

    d_keys = reduce_groups(k_sent, k_kept, near, "r_k")
    d_values = reduce_groups(v_sent, v_kept, far, "r_v")

    def key_back(dk_ref, dv_ref, raw_ref, cos_ref, sin_ref, gain_ref, out_ref, gain_out):
        d_raw, d_gain = rope_back(
            dk_ref[...], raw_ref[...], gain_ref[...], cos_ref[...], sin_ref[...]
        )
        out_ref[:, :HEAD_SIZE] = d_raw.astype(BF)
        out_ref[:, HEAD_SIZE:] = dv_ref[...].astype(BF)
        gain_out[...] = d_gain

    d_kv, d_gain_k = call(
        key_back,
        "key_back",
        [((all_rows, 2 * HEAD_SIZE), BF), ((1, HEAD_SIZE), F32)],
        [d_keys, d_values, k_raw, cosine, sine, gain_k],
    )

    def project_back(*refs):
        wq, wkv, refs = refs[:groups], refs[groups : 2 * groups], refs[2 * groups :]
        dq_ref, dkv_ref, sent_ref, kept_ref = refs
        for s in range(segments):
            at = slice(s * block, (s + 1) * block)
            for j in range(groups):
                value = dot_nt(dq_ref[at, :], wq[j][...]) + dot_nt(dkv_ref[at, :], wkv[j][...])
                store_pair(sent_ref, kept_ref, s, value, j * chunk)

    sent, kept = call(
        project_back, "project_back", pair, [*q_parts, *kv_parts, d_q, d_kv]
    )
    kept, got = scatter_rows(sent, kept, "rs4")

    q_sent, q_kept, kv_sent, kv_kept = grad_in(
        normed_all, [d_q, d_kv], [near, far], "w_qkv"
    )
    q_sums = reduce_groups(q_sent, q_kept, near, "r_q")
    kv_sums = reduce_groups(kv_sent, kv_kept, far, "r_kv")
    qkv_sums = jnp.concatenate([q_sums, kv_sums], axis=1).astype(BF)
    qkv_sums = trade(qkv_sums.reshape(4, piece, qkv_sums.shape[1]), "t_dqkv").astype(F32)
    query_grad = join(qkv_sums, 0, wide_q)
    key_grad = join(qkv_sums, wide_q, wide_q + HEAD_SIZE)
    value_grad = join(qkv_sums, wide_q + HEAD_SIZE, wide_q + 2 * HEAD_SIZE)

    def last_back(kept_ref, got_ref, x_ref, gain_ref, d_ref, out_ref, gain_out):
        grad = kept_ref[...].astype(F32) + got_ref[...].astype(F32)
        back, gain_grad = norm_back(grad, x_ref[...].astype(F32), gain_ref[...])
        out_ref[...] = (d_ref[...] + back).astype(BF)
        gain_out[...] = gain_grad

    d_x, d_gain_a = call(
        last_back,
        "norm1_back",
        [((own, width), BF), ((1, width), F32)],
        [kept, got, x_own, gain_a, d_middle],
    )
    d_x, d_gain_a, d_gain_m = put_back([d_x, d_gain_a, d_gain_m], "leave2")
    input_grad = d_x.reshape(layer_input.shape)

    gains = jnp.concatenate([d_gain_a, d_gain_m, d_gain_q, d_gain_k], axis=1).reshape(-1, 128)
    for bit in [CORE, SPLIT] + row_bits:
        gains = gains + swap(gains, bit)
    gains = (gains + swap_tp(gains)).reshape(-1)
    return (
        layer_output,
        input_grad,
        query_grad,
        key_grad,
        value_grad,
        output_grad,
        gate_grad,
        up_grad,
        down_grad,
        gains[:width],
        gains[width : 2 * width],
        gains[2 * width : 2 * width + HEAD_SIZE],
        gains[2 * width + HEAD_SIZE :],
    )


def solution(mesh):
    rows_in = P(None, "dp", "tp", None)
    in_specs = (
        rows_in,
        P("dp", "tp"),
        P("dp", "tp"),
        P("dp", "tp"),
        P("tp", "dp"),
        P("dp", "tp"),
        P("dp", "tp"),
        P("tp", "dp"),
        P(),
        P(),
        P(),
        P(),
        rows_in,
    )
    out_specs = (
        rows_in,
        rows_in,
        P("dp", "tp"),
        P("dp", "tp"),
        P("dp", "tp"),
        P("tp", "dp"),
        P("dp", "tp"),
        P("dp", "tp"),
        P("tp", "dp"),
        P(),
        P(),
        P(),
        P(),
    )
    return jax.shard_map(local, mesh=mesh, in_specs=in_specs, out_specs=out_specs, check_vma=False)
```

```python
import functools

import jax
import jax.numpy as jnp
from jax import lax
from jax.experimental import pallas as pl
from jax.experimental.pallas import tpu as pltpu
from jax.sharding import PartitionSpec as P

HEAD_SIZE = 128
ROWS_DEV = 64

EPSILON = 1e-06
ROPE_BASE = 1000000.0
MASKED = -1e30

CORE = 1
SPLIT = 8

BF = jnp.bfloat16
F32 = jnp.float32
MIB = 1 << 20


def dot(left, right):
    return jnp.dot(left, right, preferred_element_type=F32)


def dot_nt(left, right):
    return lax.dot_general(left, right, (((1,), (1,)), ((), ())), preferred_element_type=F32)


def dot_tn(left, right):
    return lax.dot_general(left, right, (((0,), (0,)), ((), ())), preferred_element_type=F32)


def tables(positions, head_width):
    half_width = head_width // 2
    inverse = ROPE_BASE ** (-(jnp.arange(half_width, dtype=F32) * 2.0 / head_width))
    angles = positions.astype(F32)[:, None] * inverse[None, :]
    angles = jnp.concatenate([angles, angles], axis=-1)
    return (jnp.cos(angles), jnp.sin(angles))


LARGE = {
    "enter",
    "pack1",
    "project",
    "attend",
    "feed",
    "feed_out",
    "attend_back",
    "project_back",
    "w_down",
    "w_gate_up",
    "w_out",
    "w_qkv",
}


def call(body, name, outs, ins, ties=(), scratch=(), scalars=(), staged=False):
    scalars, ins, ties = list(scalars), list(ins), list(ties)
    if name not in LARGE:
        skip = len(scalars) + len(ins)
        return pl.pallas_call(
            lambda *refs: body(*refs[:skip], *refs[skip + len(ties) :]),
            out_shape=[jax.ShapeDtypeStruct(s, d) for s, d in outs],
            in_specs=[pl.BlockSpec(memory_space=pltpu.SMEM)] * len(scalars)
            + [pl.BlockSpec(memory_space=pltpu.VMEM)] * len(ins)
            + [pl.BlockSpec(memory_space=pl.ANY)] * len(ties),
            out_specs=[pl.BlockSpec(memory_space=pltpu.VMEM)] * len(outs),
            scratch_shapes=list(scratch),
            compiler_params=pltpu.CompilerParams(vmem_limit_bytes=16 * MIB),
            cost_estimate=pl.CostEstimate(flops=0, bytes_accessed=0, transcendentals=0),
            name=name,
        )(*scalars, *ins, *ties)
    begin, end = len(scalars), len(scalars) + len(ins)
    n_in, n_out = len(ins), len(outs)

    def kernel(*refs):
        scalar_refs, in_refs = refs[:begin], refs[begin:end]
        rest = refs[end + len(ties) :]
        out_refs, rest = rest[:n_out], rest[n_out:]
        in_vmem, out_vmem, rest = rest[:n_in], rest[n_in : n_in + n_out], rest[n_in + n_out :]
        sems, rest = rest[0], rest[1:]
        loads = [
            pltpu.make_async_copy(in_refs[n], in_vmem[n], sems.at[n]) for n in range(n_in)
        ]
        stores = [
            pltpu.make_async_copy(out_vmem[n], out_refs[n], sems.at[n_in + n])
            for n in range(n_out)
        ]
        for load in loads:
            load.start()
        waited, sent = set(), set()

        def ready(n):
            if n not in waited:
                waited.add(n)
                loads[n].wait()

        def flush(n):
            if n not in sent:
                sent.add(n)
                stores[n].start()

        if staged:
            body(ready, flush, *scalar_refs, *in_vmem, *out_vmem, *rest)
        else:
            for n in range(n_in):
                ready(n)
            body(*scalar_refs, *in_vmem, *out_vmem, *rest)
        for n in range(n_in):
            ready(n)
        for n in range(n_out):
            flush(n)
        for store in stores:
            store.wait()

    anywhere = pl.BlockSpec(memory_space=pl.ANY)
    return pl.pallas_call(
        kernel,
        out_shape=[jax.ShapeDtypeStruct(s, d) for s, d in outs],
        in_specs=[pl.BlockSpec(memory_space=pltpu.SMEM)] * begin
        + [anywhere] * (n_in + len(ties)),
        out_specs=[anywhere] * n_out,
        scratch_shapes=[pltpu.VMEM(v.shape, v.dtype) for v in ins]
        + [pltpu.VMEM(s, d) for s, d in outs]
        + [pltpu.SemaphoreType.DMA((n_in + n_out,))]
        + list(scratch),
        compiler_params=pltpu.CompilerParams(vmem_limit_bytes=60 * MIB),
        cost_estimate=pl.CostEstimate(flops=0, bytes_accessed=0, transcendentals=0),
        name=name,
    )(*scalars, *ins, *ties)


def rms(value):
    return lax.rsqrt(jnp.mean(value * value, axis=-1, keepdims=True) + EPSILON)


def flip_sign(shape):
    lane = lax.broadcasted_iota(jnp.int32, shape, 1)
    return jnp.where(lane < HEAD_SIZE // 2, -1.0, 1.0).astype(F32)


def rope(raw, gain, cosine, sine):
    scaled = raw * rms(raw) * gain
    turned = pltpu.roll(scaled, HEAD_SIZE // 2, 1) * flip_sign(scaled.shape)
    return scaled * cosine + turned * sine


def rope_back(grad, raw, gain, cosine, sine):
    swung = grad * sine
    turned = pltpu.roll(swung, HEAD_SIZE // 2, 1) * flip_sign(swung.shape)
    d_scaled = grad * cosine - turned
    scale = rms(raw)
    unit = raw * scale
    d_gain = jnp.sum(d_scaled * unit, axis=0, keepdims=True)
    d_unit = d_scaled * gain
    d_raw = scale * (d_unit - unit * jnp.mean(d_unit * unit, axis=-1, keepdims=True))
    return d_raw, d_gain


def norm_back(grad, value, gain):
    scale = rms(value)
    unit = value * scale
    d_gain = jnp.sum(grad * unit, axis=0, keepdims=True)
    d_unit = grad * gain
    return scale * (d_unit - unit * jnp.mean(d_unit * unit, axis=-1, keepdims=True)), d_gain


def assemble(pieces, out_ref, segments, rows):
    block = len(pieces) * rows
    for m, piece in enumerate(pieces):
        for s in range(segments):
            out_ref[s * block + m * rows : s * block + (m + 1) * rows, :] = piece[
                s * rows : (s + 1) * rows, :
            ]


def local(
    layer_input,
    query_weight,
    key_matrix,
    value_matrix,
    output_weight,
    gate_weight,
    up_weight,
    down_weight,
    attn_gain,
    mlp_gain,
    query_gain,
    key_gain,
    cotangent,
):
    ways = lax.axis_size("dp")
    place = lax.axis_index("dp")
    side = lax.axis_index("tp")
    segments, _, rows, width = layer_input.shape
    piece = width // ways
    row_bits = [1 << k for k in range(ways.bit_length() - 1) if (1 << k) not in (CORE, SPLIT)]
    near, far = row_bits, row_bits[::-1]
    groups = 1 << len(row_bits)
    chunk = 4 * piece
    block = 8 * rows
    half = 4 * rows
    all_rows = segments * block
    own = segments * rows
    scale = HEAD_SIZE**-0.5
    wide_q = query_weight.shape[1] // 4
    heads_q = wide_q // HEAD_SIZE
    wide_f = gate_weight.shape[1] // 4

    def mix_list(order):
        mixes = [0]
        for bit in reversed(order):
            mixes = mixes + [mix | bit for mix in mixes]
        return mixes

    mixes = mix_list(near)
    slot = {mix: j for j, mix in enumerate(mixes)}
    quads = [[mix | CORE * (n & 1) | SPLIT * (n >> 1) for n in range(4)] for mix in mixes]
    local_order = [k for four in quads for k in four]

    def swap(value, bit):
        with jax.named_scope("swap%d" % bit):
            return lax.ppermute(value, "dp", [(i, i ^ bit) for i in range(ways)])

    def swap_tp(value):
        with jax.named_scope("swaptp"):
            return lax.ppermute(value, "tp", [(0, 1), (1, 0)])

    def trade(value, name):
        with jax.named_scope(name):
            return lax.all_to_all(value, "dp", 0, 0, axis_index_groups=quads, tiled=True)

    def turn(blocks):
        for bit in row_bits:
            flag = (place & bit) != 0
            blocks = [jnp.where(flag, blocks[k ^ bit], blocks[k]) for k in range(ways)]
        return blocks

    def to_local(value):
        blocks = turn([value[..., k * piece : (k + 1) * piece] for k in range(ways)])
        return jnp.concatenate([blocks[k] for k in local_order], axis=-1)

    def from_local(value):
        where = {k: n for n, k in enumerate(local_order)}
        blocks = [value[..., where[k] * piece : (where[k] + 1) * piece] for k in range(ways)]
        return jnp.concatenate(turn(blocks), axis=-1)

    def spread(value, order, name):
        held = {0: value}
        with jax.named_scope(name):
            for bit in order:
                for mix in list(held):
                    held[mix ^ bit] = swap(held[mix], bit)
        return [held[mix] for mix in mixes]

    wide_k = 2 * HEAD_SIZE
    wide_1 = 2 * wide_q + wide_k

    def pack_first(q_ref, k_ref, v_ref, o_ref, out_ref):
        for n in range(4):
            out_ref[n, :, :wide_q] = q_ref[:, n * wide_q : (n + 1) * wide_q]
            for at, ref in ((wide_q, k_ref), (wide_q + HEAD_SIZE, v_ref)):
                out_ref[n, :, at : at + HEAD_SIZE] = ref[:, n * HEAD_SIZE : (n + 1) * HEAD_SIZE]
            for b in range(0, wide_q, piece):
                at = wide_q + wide_k + b
                out_ref[n, :, at : at + piece] = o_ref[n * wide_q + b : n * wide_q + b + piece, :]

    def pack_columns(ref, out_ref):
        for n in range(4):
            out_ref[n] = ref[:, n * wide_f : (n + 1) * wide_f]

    (packed,) = call(
        pack_first,
        "pack1",
        [((4, piece, wide_1), BF)],
        [query_weight, key_matrix, value_matrix, output_weight],
    )
    wide_shape = ((4, piece, wide_f), BF)
    first_packed = packed
    first = trade(packed, "t_first").reshape(chunk, wide_1)

    def gather_rows(value, name):
        held = [value]
        with jax.named_scope(name):
            held = held + [swap(v, SPLIT) for v in held]
            held = held + [swap_tp(v) for v in held]
            return held + [swap(v, CORE) for v in held]

    def add_split(kept, got, name, ties=()):
        count = kept.shape[1] // 2

        def body(kept_ref, got_ref, sent_out, kept_out):
            total = kept_ref[...].astype(F32) + got_ref[...].astype(F32)
            kept_out[...] = total[:, :count].astype(BF)
            sent_out[...] = total[:, count:].astype(BF)

        shape = (segments, count, width)
        return call(body, name, [(shape, BF), (shape, BF)], [kept, got], ties=ties)

    def scatter_rows(sent, kept, name, ties_c=(), ties_t=()):
        with jax.named_scope(name):
            sent, kept = add_split(kept, swap(sent, CORE), name + "_c", ties_c)
            sent, kept = add_split(kept, swap_tp(sent), name + "_t", ties_t)
            return kept.reshape(own, width), swap(sent, SPLIT).reshape(own, width)

    pair = [((segments, half, width), BF)] * 2

    def store_pair(sent_ref, kept_ref, s, value, at):
        stop = at + value.shape[1]
        kept_ref[s, :, at:stop] = value[:half].astype(BF)
        sent_ref[s, :, at:stop] = value[half:].astype(BF)

    index = jnp.arange(all_rows, dtype=jnp.int32)
    segment_by = index // block
    m_by = (index // rows) % 8

    def positions(base):
        at = base ^ ((m_by & 1) * SPLIT) ^ ((m_by >> 2) * CORE)
        return (
            (segment_by * ways + at) * ROWS_DEV
            + (side ^ ((m_by >> 1) & 1)) * rows
            + index % rows
        )

    query_pos = positions(place)
    cosine, sine = tables(query_pos, HEAD_SIZE)
    qpos = query_pos[:, None]
    kpos = jnp.stack([positions(place ^ mix).reshape(segments, block) for mix in mixes], axis=1)
    kpos = kpos.reshape(1, segments * groups * block)
    span = min(groups, 2)

    gain_q, gain_k = query_gain[None], key_gain[None]
    row_mask = ways - 1 - CORE - SPLIT
    where = (place & row_mask)[None]

    def lanes_of(where_ref, n):
        return pl.ds(pl.multiple_of((local_order[n] ^ where_ref[0]) * piece, piece), piece)

    def enter(where_ref, x_ref, c_ref, ga_ref, gm_ref, x_out, c_out, ga_out, gm_out, out_ref):
        for n in range(ways):
            lanes, here = lanes_of(where_ref, n), slice(n * piece, (n + 1) * piece)
            x_out[:, here] = x_ref[:, lanes]
            c_out[:, here] = c_ref[:, lanes]
            ga_out[:, here] = ga_ref[:, lanes]
            gm_out[:, here] = gm_ref[:, lanes]
        value = x_out[...].astype(F32)
        out_ref[...] = (value * rms(value) * ga_out[...]).astype(BF)

    own_shape, line_shape = (own, width), (1, width)
    if piece % 128 == 0:
        x_own, c_own, gain_a, gain_m, normed = call(
            enter,
            "enter",
            [
                (own_shape, BF),
                (own_shape, BF),
                (line_shape, F32),
                (line_shape, F32),
                (own_shape, BF),
            ],
            [
                layer_input.reshape(own_shape),
                cotangent.reshape(own_shape),
                attn_gain[None],
                mlp_gain[None],
            ],
            scalars=[where],
            ties=[first_packed],
        )
    else:
        x_own = to_local(layer_input.reshape(own_shape))
        c_own = to_local(cotangent.reshape(own_shape))
        gain_a = to_local(attn_gain[None])
        gain_m = to_local(mlp_gain[None])

        def first_norm(x_ref, gain_ref, out_ref):
            value = x_ref[...].astype(F32)
            out_ref[...] = (value * rms(value) * gain_ref[...]).astype(BF)

        (normed,) = call(first_norm, "norm1", [(own_shape, BF)], [x_own, gain_a])

    def put_back(values, name, ties=()):
        if piece % 128:
            return [from_local(v) for v in values]

        def body(*refs):
            where_ref, ins, outs = refs[0], refs[1 : 1 + len(values)], refs[1 + len(values) :]
            for in_ref, out_ref in zip(ins, outs):
                for n in range(ways):
                    out_ref[:, lanes_of(where_ref, n)] = in_ref[:, n * piece : (n + 1) * piece]

        outs = [(v.shape, v.dtype) for v in values]
        return call(body, name, outs, values, scalars=[where], ties=ties)

    normed_parts = gather_rows(normed, "g_norm1")
    (packed,) = call(pack_columns, "pack2", [wide_shape], [gate_weight], ties=[first, normed_parts[1]])
    gate = trade(packed, "t_gate").reshape(chunk, wide_f)
    (packed,) = call(pack_columns, "pack3", [wide_shape], [up_weight], ties=[gate])
    up = trade(packed, "t_up").reshape(chunk, wide_f)
    down = trade(down_weight.reshape(4, wide_f, piece), "t_down")
    q_parts = spread(first[:, :wide_q], near, "s_q")
    kv_parts = spread(first[:, wide_q : wide_q + wide_k], far, "s_kv")
    o_parts = spread(first[:, wide_q + wide_k :], near, "s_o")
    gate_parts = spread(gate, near, "s_gate")
    up_parts = spread(up, far, "s_up")
    down_parts = spread(down, near, "s_down")
    c_parts = gather_rows(c_own, "g_cot")

    def project(*refs):
        parts, refs = refs[:8], refs[8:]
        wq, wkv, refs = refs[:groups], refs[groups : 2 * groups], refs[2 * groups :]
        cos_ref, sin_ref, gq_ref, gk_ref, x_ref, q_ref, kv_ref, q_raw_ref, k_raw_ref = refs
        assemble(parts, x_ref, segments, rows)
        for s in range(segments):
            at = slice(s * block, (s + 1) * block)
            q = sum(dot(x_ref[at, j * chunk : (j + 1) * chunk], wq[j][...]) for j in range(groups))
            kv = sum(
                dot(x_ref[at, j * chunk : (j + 1) * chunk], wkv[j][...]) for j in range(groups)
            )
            q_raw_ref[at, :] = q
            k_raw_ref[at, :] = kv[:, :HEAD_SIZE]
            cos, sin = cos_ref[at, :], sin_ref[at, :]
            for h in range(heads_q):
                lanes = slice(h * HEAD_SIZE, (h + 1) * HEAD_SIZE)
                q_ref[at, lanes] = rope(q[:, lanes], gq_ref[...], cos, sin).astype(BF)
            kv_ref[at, :HEAD_SIZE] = rope(kv[:, :HEAD_SIZE], gk_ref[...], cos, sin).astype(BF)
            kv_ref[at, HEAD_SIZE:] = kv[:, HEAD_SIZE:].astype(BF)

    normed_all, q, kv, q_raw, k_raw = call(
        project,
        "project",
        [
            ((all_rows, width), BF),
            ((all_rows, wide_q), BF),
            ((all_rows, 2 * HEAD_SIZE), BF),
            ((all_rows, wide_q), F32),
            ((all_rows, HEAD_SIZE), F32),
        ],
        [*normed_parts, *q_parts, *kv_parts, cosine, sine, gain_q, gain_k],
        ties=[gate],
    )
    kv_all = spread(kv, near, "s_keys")

    def load_keys(parts, scratch):
        for j, part in enumerate(parts):
            for s in range(segments):
                scratch[s * groups + j] = part[s * block : (s + 1) * block, :]

    def stack_heads(ref, s):
        at = slice(s * block, (s + 1) * block)
        return jnp.concatenate(
            [ref[at, h * HEAD_SIZE : (h + 1) * HEAD_SIZE] for h in range(heads_q)], axis=0
        )

    def load_out_weight(parts, scratch):
        for j, part in enumerate(parts):
            for n in range(4):
                at = (4 * j + n) * piece
                for b in range(0, wide_q, piece):
                    scratch[b : b + piece, at : at + piece] = part[
                        n * piece : (n + 1) * piece, b : b + piece
                    ]

    def load_down_weight(parts, scratch):
        for j, part in enumerate(parts):
            for n in range(4):
                at = (4 * j + n) * piece
                scratch[:, at : at + piece] = part[n]

    strip = min(chunk * groups, 512)

    def attend(*refs):
        kv_refs, wo, refs = refs[:groups], refs[groups : 2 * groups], refs[2 * groups :]
        q_ref, qpos_ref, kpos_ref, out_ref, lse_ref, sent_ref, kept_ref, keys, w_out = refs
        load_keys(kv_refs, keys)
        load_out_weight(wo, w_out)
        for s in range(segments):
            at = slice(s * block, (s + 1) * block)
            q = stack_heads(q_ref, s)
            pos = jnp.concatenate([qpos_ref[at, :]] * heads_q, axis=0)

            high = jnp.full((q.shape[0], 1), MASKED, F32)
            summed = jnp.zeros((q.shape[0], 1), F32)
            acc = jnp.zeros((q.shape[0], HEAD_SIZE), F32)
            for n in range(0, (s + 1) * groups, span):
                both = keys[n : n + span].reshape(span * block, 2 * HEAD_SIZE)
                scores = dot_nt(q, both[:, :HEAD_SIZE]) * scale
                key_at = kpos_ref[:, n * block : (n + span) * block]
                scores = jnp.where(key_at <= pos, scores, MASKED)
                top = jnp.maximum(high, jnp.max(scores, axis=-1, keepdims=True))
                shrink = jnp.exp(high - top)
                probs = jnp.exp(scores - top)
                summed = summed * shrink + jnp.sum(probs, axis=-1, keepdims=True)
                acc = acc * shrink + dot(probs.astype(BF), both[:, HEAD_SIZE:])
                high = top
            acc = acc / summed
            lse_ref[s] = high + jnp.log(summed)
            acc = jnp.concatenate(
                [acc[h * block : (h + 1) * block] for h in range(heads_q)], axis=1
            )
            out_ref[at, :] = acc
            heads = acc.astype(BF)
            for n in range(0, width, strip):
                store_pair(sent_ref, kept_ref, s, dot(heads, w_out[:, n : n + strip]), n)

    attended, lse, sent, kept = call(
        attend,
        "attend",
        [
            ((all_rows, wide_q), F32),
            ((segments, heads_q * block, 1), F32),
            *pair,
        ],
        [*kv_all, *o_parts, q, qpos, kpos],
        ties=[up],
        scratch=[
            pltpu.VMEM((segments * groups, block, 2 * HEAD_SIZE), BF),
            pltpu.VMEM((wide_q, width), BF),
        ],
    )
    kept, got = scatter_rows(
        sent, kept, "rs1", [gate_parts[slot[near[0]]]], [down, c_parts[1], gate_parts[slot[far[0]]]]
    )

    def second_norm(x_ref, kept_ref, got_ref, gain_ref, mid_ref, out_ref):
        value = x_ref[...].astype(F32) + (
            kept_ref[...].astype(F32) + got_ref[...].astype(F32)
        )
        mid_ref[...] = value
        out_ref[...] = (value * rms(value) * gain_ref[...]).astype(BF)

    middle, normed2 = call(
        second_norm,
        "norm2",
        [((own, width), F32), ((own, width), BF)],
        [x_own, kept, got, gain_m],
        ties=[*c_parts, *gate_parts, up_parts[slot[far[0]]]],
    )
    normed2_parts = gather_rows(normed2, "g_norm2")

    def feed(*refs):
        parts, c_refs, refs = refs[:8], refs[8:16], refs[16:]
        wg, wu, wd = refs[:groups], refs[groups : 2 * groups], refs[2 * groups : 3 * groups]
        (
            x_ref,
            c_ref,
            active_ref,
            dg_ref,
            du_ref,
            sent_ref,
            kept_ref,
            w_down,
        ) = refs[3 * groups :]
        assemble(parts, x_ref, segments, rows)
        assemble(c_refs, c_ref, segments, rows)
        load_down_weight(wd, w_down)

        for s in range(segments):
            at = slice(s * block, (s + 1) * block)
            gate_pre = sum(
                dot(x_ref[at, j * chunk : (j + 1) * chunk], wg[j][...]) for j in range(groups)
            )
            up_pre = sum(
                dot(x_ref[at, j * chunk : (j + 1) * chunk], wu[j][...]) for j in range(groups)
            )
            sigma = jax.nn.sigmoid(gate_pre)
            swish = gate_pre * sigma
            active_ref[at, :] = (swish * up_pre).astype(BF)
            d_active = dot_nt(c_ref[at, :], w_down[...])
            d_gate = (d_active * up_pre * sigma * (1.0 + gate_pre * (1.0 - sigma))).astype(BF)
            d_upper = (d_active * swish).astype(BF)
            dg_ref[at, :] = d_gate
            du_ref[at, :] = d_upper
            for j in range(groups):
                value = dot_nt(d_gate, wg[j][...]) + dot_nt(d_upper, wu[j][...])
                lanes = slice(j * chunk, (j + 1) * chunk)
                kept_ref[s, :, lanes] = value[:half].astype(BF)
                sent_ref[s, :, lanes] = value[half:].astype(BF)

    normed2_all, c_all, active, d_gate, d_upper, sent, kept = call(
        feed,
        "feed",
        [
            ((all_rows, width), BF),
            ((all_rows, width), BF),
            ((all_rows, wide_f), BF),
            ((all_rows, wide_f), BF),
            ((all_rows, wide_f), BF),
            *pair,
        ],
        [*normed2_parts, *c_parts, *gate_parts, *up_parts, *down_parts],
        scratch=[pltpu.VMEM((wide_f, width), BF)],
    )
    kept, got = scatter_rows(sent, kept, "rs2")

    def grad_in(x_all, grads, orders, name, ties=()):
        lists = [mix_list(order) for order in orders]

        def body(*refs):
            x_ref, g_refs, outs = refs[0], refs[1 : 1 + len(grads)], refs[1 + len(grads) :]
            for g_ref, mix, n in zip(g_refs, lists, range(len(grads))):
                for at, which in enumerate(mix):
                    j = slot[which]
                    value = dot_tn(x_ref[:, j * chunk : (j + 1) * chunk], g_ref[...]).astype(BF)
                    if at < groups // 2:
                        outs[2 * n + 1][at] = value
                    else:
                        outs[2 * n][at - groups // 2] = value

        outs = []
        for g in grads:
            outs += [((groups // 2, chunk, g.shape[1]), BF)] * 2
        return call(body, name, outs, [x_all, *grads], ties=ties)

    def grad_out(left, c_value, order, name):
        mix = mix_list(order)
        tall = left.shape[1]

        def body(left_ref, c_ref, sent_ref, kept_ref):
            for at, which in enumerate(mix):
                j = slot[which]
                value = dot_tn(
                    left_ref[...].astype(BF), c_ref[:, j * chunk : (j + 1) * chunk]
                ).astype(BF)
                for n in range(4):
                    part = value[:, n * piece : (n + 1) * piece]
                    if at < groups // 2:
                        kept_ref[at, n] = part
                    else:
                        sent_ref[at - groups // 2, n] = part

        return call(
            body, name, [((groups // 2, 4, tall, piece), BF)] * 2, [left, c_value]
        )

    def reduce_to_pair(sent, kept, order, name):
        with jax.named_scope(name):
            for bit in order[:-1]:
                total = kept.astype(F32) + swap(sent, bit).astype(F32)
                count = total.shape[0] // 2
                kept, sent = total[:count].astype(BF), total[count:].astype(BF)
            return kept, swap(sent, order[-1])

    def reduce_groups(sent, kept, order, name):
        kept, got = reduce_to_pair(sent, kept, order, name)
        return (kept.astype(F32) + got.astype(F32))[0]

    def add_joined(pairs, name, ties):
        shape = pairs[0][0].shape[1:]
        wide = [kept.shape[-1] for kept, _ in pairs]

        def body(*refs):
            at = 0
            for n in range(len(pairs)):
                value = refs[2 * n][0].astype(F32) + refs[2 * n + 1][0].astype(F32)
                refs[-1][..., at : at + wide[n]] = value.astype(BF)
                at += wide[n]

        ins = [v for pair in pairs for v in pair]
        return call(body, name, [((*shape[:-1], sum(wide)), BF)], ins, ties=ties)[0]

    down_sent, down_kept = grad_out(active, c_all, near, "w_down")
    down_sums = reduce_groups(down_sent, down_kept, near, "r_down")
    gate_sent, gate_kept, up_sent, up_kept = grad_in(
        normed2_all, [d_gate, d_upper], [near, far], "w_gate_up"
    )
    gate_pair = reduce_to_pair(gate_sent, gate_kept, near, "r_gate")
    up_pair = reduce_to_pair(up_sent, up_kept, far, "r_up")
    down_grad = trade(down_sums.astype(BF), "t_ddown").astype(F32).reshape(4 * wide_f, piece)
    def norm_step_back(kept_ref, got_ref, mid_ref, gain_ref, c_ref, d_ref, low_ref, gain_out):
        grad = kept_ref[...].astype(F32) + got_ref[...].astype(F32)
        back, gain_grad = norm_back(grad, mid_ref[...], gain_ref[...])
        total = c_ref[...].astype(F32) + back
        d_ref[...] = total
        low_ref[...] = total.astype(BF)
        gain_out[...] = gain_grad

    d_middle, d_branch, d_gain_m = call(
        norm_step_back,
        "norm2_back",
        [((own, width), F32), ((own, width), BF), ((1, width), F32)],
        [kept, got, middle, gain_m, c_own],
        ties=[gate_sent, down_sent],
    )
    d_parts = gather_rows(d_branch, "g_branch")

    def feed_out(*refs):
        wd, refs = refs[:groups], refs[groups:]
        active_ref, sent_ref, kept_ref, w_down = refs
        load_down_weight(wd, w_down)
        for s in range(segments):
            at = slice(s * block, (s + 1) * block)
            for n in range(0, width, strip):
                store_pair(
                    sent_ref, kept_ref, s, dot(active_ref[at, :], w_down[:, n : n + strip]), n
                )

    out_sent, out_kept = call(
        feed_out,
        "feed_out",
        pair,
        [*down_parts, active],
        ties=[],
        scratch=[pltpu.VMEM((wide_f, width), BF)],
    )
    with jax.named_scope("rs3"):
        out_sent, out_kept = add_split(out_kept, swap(out_sent, CORE), "rs3_c")
        out_got = swap_tp(out_sent)

    key_mix, value_mix = mix_list(near), mix_list(far)

    def attend_back(*refs):
        parts, kv_refs, wo = refs[:8], refs[8 : 8 + groups], refs[8 + groups : 8 + 2 * groups]
        (
            q_ref,
            qpos_ref,
            kpos_ref,
            out_ref,
            lse_ref,
            q_raw_ref,
            cos_ref,
            sin_ref,
            gq_ref,
            d_all_ref,
            dq_ref,
            gain_out,
            k_sent,
            k_kept,
            v_sent,
            v_kept,
            o_sent,
            o_kept,
            keys,
            w_out,
            sums,
        ) = refs[8 + 2 * groups :]
        out_mix = mix_list(near)
        assemble(parts, d_all_ref, segments, rows)
        load_keys(kv_refs, keys)
        load_out_weight(wo, w_out)
        sums[...] = jnp.zeros_like(sums)
        gain_total = jnp.zeros((1, HEAD_SIZE), F32)
        for s in range(segments):
            at = slice(s * block, (s + 1) * block)
            q = stack_heads(q_ref, s)
            out = stack_heads(out_ref, s)
            d_heads = dot_nt(d_all_ref[at, :], w_out[...]).astype(BF)
            grad = jnp.concatenate(
                [d_heads[:, h * HEAD_SIZE : (h + 1) * HEAD_SIZE] for h in range(heads_q)], axis=0
            )
            delta = jnp.sum(out * grad.astype(F32), axis=-1, keepdims=True)
            lse = lse_ref[s]
            pos = jnp.concatenate([qpos_ref[at, :]] * heads_q, axis=0)

            dq = jnp.zeros((q.shape[0], HEAD_SIZE), F32)
            for n in range(0, (s + 1) * groups, span):
                both = keys[n : n + span].reshape(span * block, 2 * HEAD_SIZE)
                key = both[:, :HEAD_SIZE]
                scores = dot_nt(q, key) * scale
                key_at = kpos_ref[:, n * block : (n + span) * block]
                scores = jnp.where(key_at <= pos, scores, MASKED)
                probs = jnp.exp(scores - lse)
                d_probs = dot_nt(grad, both[:, HEAD_SIZE:])
                d_scores = (probs * (d_probs - delta)).astype(BF)
                d_keys = dot_tn(d_scores, q) * scale
                d_values = dot_tn(probs.astype(BF), grad)
                both = jnp.concatenate([d_keys, d_values], axis=1)
                both = both.reshape(span, block, 2 * HEAD_SIZE)
                sums[n : n + span] = sums[n : n + span] + both
                dq = dq + dot(d_scores, key)
            dq = dq * scale
            for h in range(heads_q):
                lanes = slice(h * HEAD_SIZE, (h + 1) * HEAD_SIZE)
                d_raw, d_gain = rope_back(
                    dq[h * block : (h + 1) * block],
                    q_raw_ref[at, lanes],
                    gq_ref[...],
                    cos_ref[at, :],
                    sin_ref[at, :],
                )
                dq_ref[at, lanes] = d_raw.astype(BF)
                gain_total = gain_total + d_gain
        gain_out[...] = gain_total
        for mix, lane, sent_ref, kept_ref in (
            (key_mix, 0, k_sent, k_kept),
            (value_mix, HEAD_SIZE, v_sent, v_kept),
        ):
            for n, which in enumerate(mix):
                for s in range(segments):
                    value = sums[s * groups + slot[which], :, lane : lane + HEAD_SIZE].astype(BF)
                    rows_at = slice(s * block, (s + 1) * block)
                    if n < groups // 2:
                        kept_ref[n, rows_at, :] = value
                    else:
                        sent_ref[n - groups // 2, rows_at, :] = value
        heads = out_ref[...].astype(BF)
        for n, which in enumerate(out_mix):
            j = slot[which]
            value = dot_tn(heads, d_all_ref[:, j * chunk : (j + 1) * chunk]).astype(BF)
            for f in range(4):
                part = value[:, f * piece : (f + 1) * piece]
                if n < groups // 2:
                    o_kept[n, f] = part
                else:
                    o_sent[n - groups // 2, f] = part

    part_shape = ((groups // 2, all_rows, HEAD_SIZE), BF)
    o_shape = ((groups // 2, 4, wide_q, piece), BF)
    d_all, d_q, d_gain_q, k_sent, k_kept, v_sent, v_kept, o_sent, o_kept = call(
        attend_back,
        "attend_back",
        [
            ((all_rows, width), BF),
            ((all_rows, wide_q), BF),
            ((1, HEAD_SIZE), F32),
            part_shape,
            part_shape,
            part_shape,
            part_shape,
            o_shape,
            o_shape,
        ],
        [
            *d_parts,
            *kv_all,
            *o_parts,
            q,
            qpos,
            kpos,
            attended,
            lse,
            q_raw,
            cosine,
            sine,
            gain_q,
        ],
        ties=[out_sent],
        scratch=[
            pltpu.VMEM((segments * groups, block, 2 * HEAD_SIZE), BF),
            pltpu.VMEM((wide_q, width), BF),
            pltpu.VMEM((segments * groups, block, 2 * HEAD_SIZE), F32),
        ],
    )

    out_pair = reduce_to_pair(o_sent, o_kept, near, "r_out")

    with jax.named_scope("rs3"):
        out_sent, out_kept = add_split(out_kept, out_got, "rs3_t", [k_sent])
        out_kept, out_got = out_kept.reshape(own, width), swap(out_sent, SPLIT)
        out_got = out_got.reshape(own, width)
    d_keys = reduce_groups(k_sent, k_kept, near, "r_k")
    d_values = reduce_groups(v_sent, v_kept, far, "r_v")

    gate_up_sums = add_joined([gate_pair, up_pair], "sum_gu", [k_sent])
    gate_up = trade(gate_up_sums.reshape(4, piece, 2 * wide_f), "t_dgu")

    def key_back(dk_ref, dv_ref, raw_ref, cos_ref, sin_ref, gain_ref, out_ref, gain_out):
        d_raw, d_gain = rope_back(
            dk_ref[...], raw_ref[...], gain_ref[...], cos_ref[...], sin_ref[...]
        )
        out_ref[:, :HEAD_SIZE] = d_raw.astype(BF)
        out_ref[:, HEAD_SIZE:] = dv_ref[...].astype(BF)
        gain_out[...] = d_gain

    d_kv, d_gain_k = call(
        key_back,
        "key_back",
        [((all_rows, 2 * HEAD_SIZE), BF), ((1, HEAD_SIZE), F32)],
        [d_keys, d_values, k_raw, cosine, sine, gain_k],
        ties=[o_sent, out_sent, gate_up_sums],
    )

    def project_back(*refs):
        wq, wkv, refs = refs[:groups], refs[groups : 2 * groups], refs[2 * groups :]
        dq_ref, dkv_ref, x_ref, gain_ref, sent_ref, kept_ref, gain_out, *outs = refs
        for n, (g_ref, order) in enumerate(((dq_ref, near), (dkv_ref, far))):
            for at, which in enumerate(mix_list(order)):
                j = slot[which]
                value = dot_tn(x_ref[:, j * chunk : (j + 1) * chunk], g_ref[...]).astype(BF)
                if at < groups // 2:
                    outs[2 * n + 1][at] = value
                else:
                    outs[2 * n][at - groups // 2] = value
        for j in range(groups):
            lanes = slice(j * chunk, (j + 1) * chunk)
            gain_sum = jnp.zeros((1, chunk), F32)
            for s in range(segments):
                at = slice(s * block, (s + 1) * block)
                value = dot_nt(dq_ref[at, :], wq[j][...]) + dot_nt(dkv_ref[at, :], wkv[j][...])
                store_pair(sent_ref, kept_ref, s, value, j * chunk)
                gain_sum = gain_sum + jnp.sum(
                    value * x_ref[at, lanes].astype(F32), axis=0, keepdims=True
                )
            gain_out[:, lanes] = gain_sum / gain_ref[:, lanes]

    sent, kept, d_gain_a, q_sent, q_kept, kv_sent, kv_kept = call(
        project_back,
        "project_back",
        [
            *pair,
            (line_shape, F32),
            *[((groups // 2, chunk, wide_q), BF)] * 2,
            *[((groups // 2, chunk, 2 * HEAD_SIZE), BF)] * 2,
        ],
        [*q_parts, *kv_parts, d_q, d_kv, normed_all, gain_a],
    )
    with jax.named_scope("rs4"):
        got = swap(sent, CORE)
    with jax.named_scope("rs4"):
        sent, kept = add_split(kept, got, "rs4_c")
        got = swap_tp(sent)
    with jax.named_scope("rs4"):
        sent, kept = add_split(kept, got, "rs4_t")
        kept, got = kept.reshape(own, width), swap(sent, SPLIT).reshape(own, width)
    q_pair = reduce_to_pair(q_sent, q_kept, near, "r_q")
    kv_pair = reduce_to_pair(kv_sent, kv_kept, far, "r_kv")
    qkv_sums = add_joined([q_pair, kv_pair], "sum_qkv", [sent, gate_up])
    out_sums = add_joined([out_pair], "sum_out", [sent, gate_up])
    output_grad = trade(out_sums, "t_dout").astype(F32).reshape(4 * wide_q, piece)
    qkv_sums = trade(qkv_sums.reshape(4, piece, qkv_sums.shape[1]), "t_dqkv").astype(F32)

    def join(value, start, stop):
        return jnp.concatenate([value[n, :, start:stop] for n in range(4)], axis=1)

    gate_up = gate_up.astype(F32)
    gate_grad = join(gate_up, 0, wide_f)
    up_grad = join(gate_up, wide_f, 2 * wide_f)
    query_grad = join(qkv_sums, 0, wide_q)
    key_grad = join(qkv_sums, wide_q, wide_q + HEAD_SIZE)
    value_grad = join(qkv_sums, wide_q + HEAD_SIZE, wide_q + 2 * HEAD_SIZE)

    layer_output = (middle + (out_kept.astype(F32) + out_got.astype(F32))).astype(BF)
    layer_output = put_back([layer_output], "leave1", [sent])[0].reshape(layer_input.shape)

    def last_back(kept_ref, got_ref, x_ref, gain_ref, d_ref, out_ref):
        grad = kept_ref[...].astype(F32) + got_ref[...].astype(F32)
        back, _ = norm_back(grad, x_ref[...].astype(F32), gain_ref[...])
        out_ref[...] = (d_ref[...] + back).astype(BF)

    (d_x,) = call(
        last_back,
        "norm1_back",
        [((own, width), BF)],
        [kept, got, x_own, gain_a, d_middle],
    )
    input_grad = put_back([d_x], "leave2")[0].reshape(layer_input.shape)

    d_gain_a, d_gain_m = put_back([d_gain_a, d_gain_m], "leave3", [got])
    gains = jnp.concatenate([d_gain_a, d_gain_m, d_gain_q, d_gain_k], axis=1).reshape(-1, 128)
    for bit in [CORE] + row_bits:
        gains = gains + swap(gains, bit)
    gains = gains + swap_tp(gains)
    gains = (gains + swap(gains, SPLIT)).reshape(-1)
    return (
        layer_output,
        input_grad,
        query_grad,
        key_grad,
        value_grad,
        output_grad,
        gate_grad,
        up_grad,
        down_grad,
        gains[:width],
        gains[width : 2 * width],
        gains[2 * width : 2 * width + HEAD_SIZE],
        gains[2 * width + HEAD_SIZE :],
    )


def solution(mesh):
    rows_in = P(None, "dp", "tp", None)
    in_specs = (
        rows_in,
        P("dp", "tp"),
        P("dp", "tp"),
        P("dp", "tp"),
        P("tp", "dp"),
        P("dp", "tp"),
        P("dp", "tp"),
        P("tp", "dp"),
        P(),
        P(),
        P(),
        P(),
        rows_in,
    )
    out_specs = (
        rows_in,
        rows_in,
        P("dp", "tp"),
        P("dp", "tp"),
        P("dp", "tp"),
        P("tp", "dp"),
        P("dp", "tp"),
        P("dp", "tp"),
        P("tp", "dp"),
        P(),
        P(),
        P(),
        P(),
    )
    return jax.shard_map(local, mesh=mesh, in_specs=in_specs, out_specs=out_specs, check_vma=False)
```

```python
import functools

import jax
import jax.numpy as jnp
from jax import lax
from jax.experimental import pallas as pl
from jax.experimental.pallas import tpu as pltpu
from jax.sharding import PartitionSpec as P

HEAD_SIZE = 128
ROWS_DEV = 64

EPSILON = 1e-06
ROPE_BASE = 1000000.0
MASKED = -1e30

CORE = 1
SPLIT = 8

BF = jnp.bfloat16
F32 = jnp.float32
MIB = 1 << 20


def dot(left, right):
    return jnp.dot(left, right, preferred_element_type=F32)


def dot_nt(left, right):
    return lax.dot_general(left, right, (((1,), (1,)), ((), ())), preferred_element_type=F32)


def dot_tn(left, right):
    return lax.dot_general(left, right, (((0,), (0,)), ((), ())), preferred_element_type=F32)


def tables(positions, head_width):
    half_width = head_width // 2
    inverse = ROPE_BASE ** (-(jnp.arange(half_width, dtype=F32) * 2.0 / head_width))
    angles = positions.astype(F32)[:, None] * inverse[None, :]
    angles = jnp.concatenate([angles, angles], axis=-1)
    return (jnp.cos(angles), jnp.sin(angles))


LARGE = {
    "enter",
    "pack1",
    "project",
    "attend",
    "feed",
    "feed_out",
    "attend_back",
    "project_back",
    "w_down",
    "w_gate_up",
    "w_out",
    "w_qkv",
}


def call(body, name, outs, ins, ties=(), scratch=(), scalars=(), staged=False):
    scalars, ins, ties = list(scalars), list(ins), list(ties)
    if name not in LARGE:
        skip = len(scalars) + len(ins)
        return pl.pallas_call(
            lambda *refs: body(*refs[:skip], *refs[skip + len(ties) :]),
            out_shape=[jax.ShapeDtypeStruct(s, d) for s, d in outs],
            in_specs=[pl.BlockSpec(memory_space=pltpu.SMEM)] * len(scalars)
            + [pl.BlockSpec(memory_space=pltpu.VMEM)] * len(ins)
            + [pl.BlockSpec(memory_space=pl.ANY)] * len(ties),
            out_specs=[pl.BlockSpec(memory_space=pltpu.VMEM)] * len(outs),
            scratch_shapes=list(scratch),
            compiler_params=pltpu.CompilerParams(vmem_limit_bytes=16 * MIB),
            cost_estimate=pl.CostEstimate(flops=0, bytes_accessed=0, transcendentals=0),
            name=name,
        )(*scalars, *ins, *ties)
    begin, end = len(scalars), len(scalars) + len(ins)
    n_in, n_out = len(ins), len(outs)

    def kernel(*refs):
        scalar_refs, in_refs = refs[:begin], refs[begin:end]
        rest = refs[end + len(ties) :]
        out_refs, rest = rest[:n_out], rest[n_out:]
        in_vmem, out_vmem, rest = rest[:n_in], rest[n_in : n_in + n_out], rest[n_in + n_out :]
        sems, rest = rest[0], rest[1:]
        loads = [
            pltpu.make_async_copy(in_refs[n], in_vmem[n], sems.at[n]) for n in range(n_in)
        ]
        stores = [
            pltpu.make_async_copy(out_vmem[n], out_refs[n], sems.at[n_in + n])
            for n in range(n_out)
        ]
        for load in loads:
            load.start()
        waited, sent = set(), set()

        def ready(n):
            if n not in waited:
                waited.add(n)
                loads[n].wait()

        def flush(n):
            if n not in sent:
                sent.add(n)
                stores[n].start()

        if staged:
            body(ready, flush, *scalar_refs, *in_vmem, *out_vmem, *rest)
        else:
            for n in range(n_in):
                ready(n)
            body(*scalar_refs, *in_vmem, *out_vmem, *rest)
        for n in range(n_in):
            ready(n)
        for n in range(n_out):
            flush(n)
        for store in stores:
            store.wait()

    anywhere = pl.BlockSpec(memory_space=pl.ANY)
    return pl.pallas_call(
        kernel,
        out_shape=[jax.ShapeDtypeStruct(s, d) for s, d in outs],
        in_specs=[pl.BlockSpec(memory_space=pltpu.SMEM)] * begin
        + [anywhere] * (n_in + len(ties)),
        out_specs=[anywhere] * n_out,
        scratch_shapes=[pltpu.VMEM(v.shape, v.dtype) for v in ins]
        + [pltpu.VMEM(s, d) for s, d in outs]
        + [pltpu.SemaphoreType.DMA((n_in + n_out,))]
        + list(scratch),
        compiler_params=pltpu.CompilerParams(vmem_limit_bytes=60 * MIB),
        cost_estimate=pl.CostEstimate(flops=0, bytes_accessed=0, transcendentals=0),
        name=name,
    )(*scalars, *ins, *ties)


def rms(value):
    return lax.rsqrt(jnp.mean(value * value, axis=-1, keepdims=True) + EPSILON)


def flip_sign(shape):
    lane = lax.broadcasted_iota(jnp.int32, shape, 1)
    return jnp.where(lane < HEAD_SIZE // 2, -1.0, 1.0).astype(F32)


def rope(raw, gain, cosine, sine):
    scaled = raw * rms(raw) * gain
    turned = pltpu.roll(scaled, HEAD_SIZE // 2, 1) * flip_sign(scaled.shape)
    return scaled * cosine + turned * sine


def rope_back(grad, raw, gain, cosine, sine):
    swung = grad * sine
    turned = pltpu.roll(swung, HEAD_SIZE // 2, 1) * flip_sign(swung.shape)
    d_scaled = grad * cosine - turned
    scale = rms(raw)
    unit = raw * scale
    d_gain = jnp.sum(d_scaled * unit, axis=0, keepdims=True)
    d_unit = d_scaled * gain
    d_raw = scale * (d_unit - unit * jnp.mean(d_unit * unit, axis=-1, keepdims=True))
    return d_raw, d_gain


def norm_back(grad, value, gain):
    scale = rms(value)
    unit = value * scale
    d_gain = jnp.sum(grad * unit, axis=0, keepdims=True)
    d_unit = grad * gain
    return scale * (d_unit - unit * jnp.mean(d_unit * unit, axis=-1, keepdims=True)), d_gain


def assemble(pieces, out_ref, segments, rows):
    block = len(pieces) * rows
    for m, piece in enumerate(pieces):
        for s in range(segments):
            out_ref[s * block + m * rows : s * block + (m + 1) * rows, :] = piece[
                s * rows : (s + 1) * rows, :
            ]


def local(
    layer_input,
    query_weight,
    key_matrix,
    value_matrix,
    output_weight,
    gate_weight,
    up_weight,
    down_weight,
    attn_gain,
    mlp_gain,
    query_gain,
    key_gain,
    cotangent,
):
    ways = lax.axis_size("dp")
    place = lax.axis_index("dp")
    side = lax.axis_index("tp")
    segments, _, rows, width = layer_input.shape
    piece = width // ways
    row_bits = [1 << k for k in range(ways.bit_length() - 1) if (1 << k) not in (CORE, SPLIT)]
    near, far = row_bits, row_bits[::-1]
    groups = 1 << len(row_bits)
    chunk = 4 * piece
    block = 8 * rows
    half = 4 * rows
    all_rows = segments * block
    own = segments * rows
    scale = HEAD_SIZE**-0.5
    wide_q = query_weight.shape[1] // 4
    heads_q = wide_q // HEAD_SIZE
    wide_f = gate_weight.shape[1] // 4

    def mix_list(order):
        mixes = [0]
        for bit in reversed(order):
            mixes = mixes + [mix | bit for mix in mixes]
        return mixes

    mixes = mix_list(near)
    slot = {mix: j for j, mix in enumerate(mixes)}
    quads = [[mix | CORE * (n & 1) | SPLIT * (n >> 1) for n in range(4)] for mix in mixes]
    local_order = [k for four in quads for k in four]

    def swap(value, bit):
        with jax.named_scope("swap%d" % bit):
            return lax.ppermute(value, "dp", [(i, i ^ bit) for i in range(ways)])

    def swap_tp(value):
        with jax.named_scope("swaptp"):
            return lax.ppermute(value, "tp", [(0, 1), (1, 0)])

    def trade(value, name):
        with jax.named_scope(name):
            return lax.all_to_all(value, "dp", 0, 0, axis_index_groups=quads, tiled=True)

    def turn(blocks):
        for bit in row_bits:
            flag = (place & bit) != 0
            blocks = [jnp.where(flag, blocks[k ^ bit], blocks[k]) for k in range(ways)]
        return blocks

    def to_local(value):
        blocks = turn([value[..., k * piece : (k + 1) * piece] for k in range(ways)])
        return jnp.concatenate([blocks[k] for k in local_order], axis=-1)

    def from_local(value):
        where = {k: n for n, k in enumerate(local_order)}
        blocks = [value[..., where[k] * piece : (where[k] + 1) * piece] for k in range(ways)]
        return jnp.concatenate(turn(blocks), axis=-1)

    def spread(value, order, name):
        held = {0: value}
        with jax.named_scope(name):
            for bit in order:
                for mix in list(held):
                    held[mix ^ bit] = swap(held[mix], bit)
        return [held[mix] for mix in mixes]

    wide_k = 2 * HEAD_SIZE
    wide_1 = 2 * wide_q + wide_k

    def pack_first(q_ref, k_ref, v_ref, o_ref, out_ref):
        for n in range(4):
            out_ref[n, :, :wide_q] = q_ref[:, n * wide_q : (n + 1) * wide_q]
            for at, ref in ((wide_q, k_ref), (wide_q + HEAD_SIZE, v_ref)):
                out_ref[n, :, at : at + HEAD_SIZE] = ref[:, n * HEAD_SIZE : (n + 1) * HEAD_SIZE]
            for b in range(0, wide_q, piece):
                at = wide_q + wide_k + b
                out_ref[n, :, at : at + piece] = o_ref[n * wide_q + b : n * wide_q + b + piece, :]

    def pack_columns(ref, out_ref):
        for n in range(4):
            out_ref[n] = ref[:, n * wide_f : (n + 1) * wide_f]

    (packed,) = call(
        pack_first,
        "pack1",
        [((4, piece, wide_1), BF)],
        [query_weight, key_matrix, value_matrix, output_weight],
    )
    wide_shape = ((4, piece, wide_f), BF)
    first_packed = packed
    first = trade(packed, "t_first").reshape(chunk, wide_1)

    def gather_rows(value, name):
        held = [value]
        with jax.named_scope(name):
            held = held + [swap(v, SPLIT) for v in held]
            held = held + [swap_tp(v) for v in held]
            return held + [swap(v, CORE) for v in held]

    def add_split(kept, got, name, ties=()):
        count = kept.shape[1] // 2

        def body(kept_ref, got_ref, sent_out, kept_out):
            total = kept_ref[...].astype(F32) + got_ref[...].astype(F32)
            kept_out[...] = total[:, :count].astype(BF)
            sent_out[...] = total[:, count:].astype(BF)

        shape = (segments, count, width)
        return call(body, name, [(shape, BF), (shape, BF)], [kept, got], ties=ties)

    def scatter_rows(sent, kept, name, ties_c=(), ties_t=()):
        with jax.named_scope(name):
            sent, kept = add_split(kept, swap(sent, CORE), name + "_c", ties_c)
            sent, kept = add_split(kept, swap_tp(sent), name + "_t", ties_t)
            return kept.reshape(own, width), swap(sent, SPLIT).reshape(own, width)

    pair = [((segments, half, width), BF)] * 2

    def store_pair(sent_ref, kept_ref, s, value, at):
        stop = at + value.shape[1]
        kept_ref[s, :, at:stop] = value[:half].astype(BF)
        sent_ref[s, :, at:stop] = value[half:].astype(BF)

    index = jnp.arange(all_rows, dtype=jnp.int32)
    segment_by = index // block
    m_by = (index // rows) % 8

    def positions(base):
        at = base ^ ((m_by & 1) * SPLIT) ^ ((m_by >> 2) * CORE)
        return (
            (segment_by * ways + at) * ROWS_DEV
            + (side ^ ((m_by >> 1) & 1)) * rows
            + index % rows
        )

    query_pos = positions(place)
    cosine, sine = tables(query_pos, HEAD_SIZE)
    qpos = query_pos[:, None]
    kpos = jnp.stack([positions(place ^ mix).reshape(segments, block) for mix in mixes], axis=1)
    kpos = kpos.reshape(1, segments * groups * block)
    span = min(groups, 2)

    gain_q, gain_k = query_gain[None], key_gain[None]
    row_mask = ways - 1 - CORE - SPLIT
    where = (place & row_mask)[None]

    def lanes_of(where_ref, n):
        return pl.ds(pl.multiple_of((local_order[n] ^ where_ref[0]) * piece, piece), piece)

    def enter(where_ref, x_ref, c_ref, ga_ref, gm_ref, x_out, c_out, ga_out, gm_out, out_ref):
        for n in range(ways):
            lanes, here = lanes_of(where_ref, n), slice(n * piece, (n + 1) * piece)
            x_out[:, here] = x_ref[:, lanes]
            c_out[:, here] = c_ref[:, lanes]
            ga_out[:, here] = ga_ref[:, lanes]
            gm_out[:, here] = gm_ref[:, lanes]
        value = x_out[...].astype(F32)
        out_ref[...] = (value * rms(value) * ga_out[...]).astype(BF)

    own_shape, line_shape = (own, width), (1, width)
    if piece % 128 == 0:
        x_own, c_own, gain_a, gain_m, normed = call(
            enter,
            "enter",
            [
                (own_shape, BF),
                (own_shape, BF),
                (line_shape, F32),
                (line_shape, F32),
                (own_shape, BF),
            ],
            [
                layer_input.reshape(own_shape),
                cotangent.reshape(own_shape),
                attn_gain[None],
                mlp_gain[None],
            ],
            scalars=[where],
            ties=[first_packed],
        )
    else:
        x_own = to_local(layer_input.reshape(own_shape))
        c_own = to_local(cotangent.reshape(own_shape))
        gain_a = to_local(attn_gain[None])
        gain_m = to_local(mlp_gain[None])

        def first_norm(x_ref, gain_ref, out_ref):
            value = x_ref[...].astype(F32)
            out_ref[...] = (value * rms(value) * gain_ref[...]).astype(BF)

        (normed,) = call(first_norm, "norm1", [(own_shape, BF)], [x_own, gain_a])

    def put_back(values, name, ties=()):
        if piece % 128:
            return [from_local(v) for v in values]

        def body(*refs):
            where_ref, ins, outs = refs[0], refs[1 : 1 + len(values)], refs[1 + len(values) :]
            for in_ref, out_ref in zip(ins, outs):
                for n in range(ways):
                    out_ref[:, lanes_of(where_ref, n)] = in_ref[:, n * piece : (n + 1) * piece]

        outs = [(v.shape, v.dtype) for v in values]
        return call(body, name, outs, values, scalars=[where], ties=ties)

    normed_parts = gather_rows(normed, "g_norm1")
    (packed,) = call(pack_columns, "pack2", [wide_shape], [gate_weight], ties=[first, normed_parts[1]])
    gate = trade(packed, "t_gate").reshape(chunk, wide_f)
    (packed,) = call(pack_columns, "pack3", [wide_shape], [up_weight], ties=[gate])
    up = trade(packed, "t_up").reshape(chunk, wide_f)
    down = trade(down_weight.reshape(4, wide_f, piece), "t_down")
    q_parts = spread(first[:, :wide_q], near, "s_q")
    kv_parts = spread(first[:, wide_q : wide_q + wide_k], far, "s_kv")
    o_parts = spread(first[:, wide_q + wide_k :], near, "s_o")
    gate_parts = spread(gate, near, "s_gate")
    up_parts = spread(up, far, "s_up")
    down_parts = spread(down, near, "s_down")
    c_parts = gather_rows(c_own, "g_cot")

    def project(*refs):
        parts, refs = refs[:8], refs[8:]
        wq, wkv, refs = refs[:groups], refs[groups : 2 * groups], refs[2 * groups :]
        cos_ref, sin_ref, gq_ref, gk_ref, x_ref, q_ref, kv_ref, q_raw_ref, k_raw_ref = refs
        assemble(parts, x_ref, segments, rows)
        for s in range(segments):
            at = slice(s * block, (s + 1) * block)
            q = sum(dot(x_ref[at, j * chunk : (j + 1) * chunk], wq[j][...]) for j in range(groups))
            kv = sum(
                dot(x_ref[at, j * chunk : (j + 1) * chunk], wkv[j][...]) for j in range(groups)
            )
            q_raw_ref[at, :] = q
            k_raw_ref[at, :] = kv[:, :HEAD_SIZE]
            cos, sin = cos_ref[at, :], sin_ref[at, :]
            for h in range(heads_q):
                lanes = slice(h * HEAD_SIZE, (h + 1) * HEAD_SIZE)
                q_ref[at, lanes] = rope(q[:, lanes], gq_ref[...], cos, sin).astype(BF)
            kv_ref[at, :HEAD_SIZE] = rope(kv[:, :HEAD_SIZE], gk_ref[...], cos, sin).astype(BF)
            kv_ref[at, HEAD_SIZE:] = kv[:, HEAD_SIZE:].astype(BF)

    normed_all, q, kv, q_raw, k_raw = call(
        project,
        "project",
        [
            ((all_rows, width), BF),
            ((all_rows, wide_q), BF),
            ((all_rows, 2 * HEAD_SIZE), BF),
            ((all_rows, wide_q), F32),
            ((all_rows, HEAD_SIZE), F32),
        ],
        [*normed_parts, *q_parts, *kv_parts, cosine, sine, gain_q, gain_k],
        ties=[gate],
    )
    kv_all = spread(kv, near, "s_keys")

    def load_keys(parts, scratch):
        for j, part in enumerate(parts):
            for s in range(segments):
                scratch[s * groups + j] = part[s * block : (s + 1) * block, :]

    def stack_heads(ref, s):
        at = slice(s * block, (s + 1) * block)
        return jnp.concatenate(
            [ref[at, h * HEAD_SIZE : (h + 1) * HEAD_SIZE] for h in range(heads_q)], axis=0
        )

    def load_out_weight(parts, scratch):
        for j, part in enumerate(parts):
            for n in range(4):
                at = (4 * j + n) * piece
                for b in range(0, wide_q, piece):
                    scratch[b : b + piece, at : at + piece] = part[
                        n * piece : (n + 1) * piece, b : b + piece
                    ]

    def load_down_weight(parts, scratch):
        for j, part in enumerate(parts):
            for n in range(4):
                at = (4 * j + n) * piece
                scratch[:, at : at + piece] = part[n]

    strip = min(chunk * groups, 512)

    def attend(*refs):
        kv_refs, wo, refs = refs[:groups], refs[groups : 2 * groups], refs[2 * groups :]
        q_ref, qpos_ref, kpos_ref, out_ref, lse_ref, sent_ref, kept_ref, keys, w_out = refs
        load_keys(kv_refs, keys)
        load_out_weight(wo, w_out)
        for s in range(segments):
            at = slice(s * block, (s + 1) * block)
            q = stack_heads(q_ref, s)
            pos = jnp.concatenate([qpos_ref[at, :]] * heads_q, axis=0)

            high = jnp.full((q.shape[0], 1), MASKED, F32)
            summed = jnp.zeros((q.shape[0], 1), F32)
            acc = jnp.zeros((q.shape[0], HEAD_SIZE), F32)
            for n in range(0, (s + 1) * groups, span):
                both = keys[n : n + span].reshape(span * block, 2 * HEAD_SIZE)
                scores = dot_nt(q, both[:, :HEAD_SIZE]) * scale
                key_at = kpos_ref[:, n * block : (n + span) * block]
                scores = jnp.where(key_at <= pos, scores, MASKED)
                top = jnp.maximum(high, jnp.max(scores, axis=-1, keepdims=True))
                shrink = jnp.exp(high - top)
                probs = jnp.exp(scores - top)
                summed = summed * shrink + jnp.sum(probs, axis=-1, keepdims=True)
                acc = acc * shrink + dot(probs.astype(BF), both[:, HEAD_SIZE:])
                high = top
            acc = acc / summed
            lse_ref[s] = high + jnp.log(summed)
            acc = jnp.concatenate(
                [acc[h * block : (h + 1) * block] for h in range(heads_q)], axis=1
            )
            out_ref[at, :] = acc
            heads = acc.astype(BF)
            for n in range(0, width, strip):
                store_pair(sent_ref, kept_ref, s, dot(heads, w_out[:, n : n + strip]), n)

    attended, lse, sent, kept = call(
        attend,
        "attend",
        [
            ((all_rows, wide_q), F32),
            ((segments, heads_q * block, 1), F32),
            *pair,
        ],
        [*kv_all, *o_parts, q, qpos, kpos],
        ties=[up],
        scratch=[
            pltpu.VMEM((segments * groups, block, 2 * HEAD_SIZE), BF),
            pltpu.VMEM((wide_q, width), BF),
        ],
    )
    kept, got = scatter_rows(
        sent, kept, "rs1", [gate_parts[slot[near[0]]]], [down, c_parts[1], gate_parts[slot[far[0]]]]
    )

    def second_norm(x_ref, kept_ref, got_ref, gain_ref, mid_ref, out_ref):
        value = x_ref[...].astype(F32) + (
            kept_ref[...].astype(F32) + got_ref[...].astype(F32)
        )
        mid_ref[...] = value
        out_ref[...] = (value * rms(value) * gain_ref[...]).astype(BF)

    middle, normed2 = call(
        second_norm,
        "norm2",
        [((own, width), F32), ((own, width), BF)],
        [x_own, kept, got, gain_m],
        ties=[*c_parts, *gate_parts, up_parts[slot[far[0]]]],
    )
    normed2_parts = gather_rows(normed2, "g_norm2")

    def feed(*refs):
        parts, c_refs, refs = refs[:8], refs[8:16], refs[16:]
        wg, wu, wd = refs[:groups], refs[groups : 2 * groups], refs[2 * groups : 3 * groups]
        (
            x_ref,
            c_ref,
            active_ref,
            dg_ref,
            du_ref,
            sent_ref,
            kept_ref,
            w_down,
        ) = refs[3 * groups :]
        assemble(parts, x_ref, segments, rows)
        assemble(c_refs, c_ref, segments, rows)
        load_down_weight(wd, w_down)

        for s in range(segments):
            at = slice(s * block, (s + 1) * block)
            gate_pre = sum(
                dot(x_ref[at, j * chunk : (j + 1) * chunk], wg[j][...]) for j in range(groups)
            )
            up_pre = sum(
                dot(x_ref[at, j * chunk : (j + 1) * chunk], wu[j][...]) for j in range(groups)
            )
            sigma = jax.nn.sigmoid(gate_pre)
            swish = gate_pre * sigma
            active_ref[at, :] = (swish * up_pre).astype(BF)
            d_active = dot_nt(c_ref[at, :], w_down[...])
            d_gate = (d_active * up_pre * sigma * (1.0 + gate_pre * (1.0 - sigma))).astype(BF)
            d_upper = (d_active * swish).astype(BF)
            dg_ref[at, :] = d_gate
            du_ref[at, :] = d_upper
            for j in range(groups):
                value = dot_nt(d_gate, wg[j][...]) + dot_nt(d_upper, wu[j][...])
                lanes = slice(j * chunk, (j + 1) * chunk)
                kept_ref[s, :, lanes] = value[:half].astype(BF)
                sent_ref[s, :, lanes] = value[half:].astype(BF)

    normed2_all, c_all, active, d_gate, d_upper, sent, kept = call(
        feed,
        "feed",
        [
            ((all_rows, width), BF),
            ((all_rows, width), BF),
            ((all_rows, wide_f), BF),
            ((all_rows, wide_f), BF),
            ((all_rows, wide_f), BF),
            *pair,
        ],
        [*normed2_parts, *c_parts, *gate_parts, *up_parts, *down_parts],
        scratch=[pltpu.VMEM((wide_f, width), BF)],
    )
    kept, got = scatter_rows(sent, kept, "rs2")

    def grad_in(x_all, grads, orders, name, ties=()):
        lists = [mix_list(order) for order in orders]

        def body(*refs):
            x_ref, g_refs, outs = refs[0], refs[1 : 1 + len(grads)], refs[1 + len(grads) :]
            for g_ref, mix, n in zip(g_refs, lists, range(len(grads))):
                for at, which in enumerate(mix):
                    j = slot[which]
                    value = dot_tn(x_ref[:, j * chunk : (j + 1) * chunk], g_ref[...]).astype(BF)
                    if at < groups // 2:
                        outs[2 * n + 1][at] = value
                    else:
                        outs[2 * n][at - groups // 2] = value

        outs = []
        for g in grads:
            outs += [((groups // 2, chunk, g.shape[1]), BF)] * 2
        return call(body, name, outs, [x_all, *grads], ties=ties)

    def grad_out(left, c_value, order, name):
        mix = mix_list(order)
        tall = left.shape[1]

        def body(left_ref, c_ref, sent_ref, kept_ref):
            for at, which in enumerate(mix):
                j = slot[which]
                value = dot_tn(
                    left_ref[...].astype(BF), c_ref[:, j * chunk : (j + 1) * chunk]
                ).astype(BF)
                for n in range(4):
                    part = value[:, n * piece : (n + 1) * piece]
                    if at < groups // 2:
                        kept_ref[at, n] = part
                    else:
                        sent_ref[at - groups // 2, n] = part

        return call(
            body, name, [((groups // 2, 4, tall, piece), BF)] * 2, [left, c_value]
        )

    def reduce_to_pair(sent, kept, order, name):
        with jax.named_scope(name):
            for bit in order[:-1]:
                total = kept.astype(F32) + swap(sent, bit).astype(F32)
                count = total.shape[0] // 2
                kept, sent = total[:count].astype(BF), total[count:].astype(BF)
            return kept, swap(sent, order[-1])

    def reduce_groups(sent, kept, order, name):
        kept, got = reduce_to_pair(sent, kept, order, name)
        return (kept.astype(F32) + got.astype(F32))[0]

    def add_joined(pairs, name, ties):
        shape = pairs[0][0].shape[1:]
        wide = [kept.shape[-1] for kept, _ in pairs]

        def body(*refs):
            at = 0
            for n in range(len(pairs)):
                value = refs[2 * n][0].astype(F32) + refs[2 * n + 1][0].astype(F32)
                refs[-1][..., at : at + wide[n]] = value.astype(BF)
                at += wide[n]

        ins = [v for pair in pairs for v in pair]
        return call(body, name, [((*shape[:-1], sum(wide)), BF)], ins, ties=ties)[0]

    down_sent, down_kept = grad_out(active, c_all, near, "w_down")
    down_sums = reduce_groups(down_sent, down_kept, near, "r_down")
    gate_sent, gate_kept, up_sent, up_kept = grad_in(
        normed2_all, [d_gate, d_upper], [near, far], "w_gate_up"
    )
    gate_pair = reduce_to_pair(gate_sent, gate_kept, near, "r_gate")
    up_pair = reduce_to_pair(up_sent, up_kept, far, "r_up")
    down_grad = trade(down_sums.astype(BF), "t_ddown").astype(F32).reshape(4 * wide_f, piece)
    def norm_step_back(kept_ref, got_ref, mid_ref, gain_ref, c_ref, d_ref, low_ref, gain_out):
        grad = kept_ref[...].astype(F32) + got_ref[...].astype(F32)
        back, gain_grad = norm_back(grad, mid_ref[...], gain_ref[...])
        total = c_ref[...].astype(F32) + back
        d_ref[...] = total
        low_ref[...] = total.astype(BF)
        gain_out[...] = gain_grad

    d_middle, d_branch, d_gain_m = call(
        norm_step_back,
        "norm2_back",
        [((own, width), F32), ((own, width), BF), ((1, width), F32)],
        [kept, got, middle, gain_m, c_own],
        ties=[gate_sent, down_sent],
    )
    d_parts = gather_rows(d_branch, "g_branch")

    def feed_out(*refs):
        wd, refs = refs[:groups], refs[groups:]
        active_ref, sent_ref, kept_ref, w_down = refs
        load_down_weight(wd, w_down)
        for s in range(segments):
            at = slice(s * block, (s + 1) * block)
            for n in range(0, width, strip):
                store_pair(
                    sent_ref, kept_ref, s, dot(active_ref[at, :], w_down[:, n : n + strip]), n
                )

    out_sent, out_kept = call(
        feed_out,
        "feed_out",
        pair,
        [*down_parts, active],
        ties=[],
        scratch=[pltpu.VMEM((wide_f, width), BF)],
    )
    with jax.named_scope("rs3"):
        out_sent, out_kept = add_split(out_kept, swap(out_sent, CORE), "rs3_c")
        out_got = swap_tp(out_sent)

    key_mix, value_mix = mix_list(near), mix_list(far)

    def attend_back(*refs):
        parts, kv_refs, wo = refs[:8], refs[8 : 8 + groups], refs[8 + groups : 8 + 2 * groups]
        (
            q_ref,
            qpos_ref,
            kpos_ref,
            out_ref,
            lse_ref,
            q_raw_ref,
            cos_ref,
            sin_ref,
            gq_ref,
            d_all_ref,
            dq_ref,
            gain_out,
            k_sent,
            k_kept,
            v_sent,
            v_kept,
            o_sent,
            o_kept,
            keys,
            w_out,
            sums,
        ) = refs[8 + 2 * groups :]
        out_mix = mix_list(near)
        assemble(parts, d_all_ref, segments, rows)
        load_keys(kv_refs, keys)
        load_out_weight(wo, w_out)
        sums[...] = jnp.zeros_like(sums)
        gain_total = jnp.zeros((1, HEAD_SIZE), F32)
        for s in range(segments):
            at = slice(s * block, (s + 1) * block)
            q = stack_heads(q_ref, s)
            out = stack_heads(out_ref, s)
            d_heads = dot_nt(d_all_ref[at, :], w_out[...]).astype(BF)
            grad = jnp.concatenate(
                [d_heads[:, h * HEAD_SIZE : (h + 1) * HEAD_SIZE] for h in range(heads_q)], axis=0
            )
            delta = jnp.sum(out * grad.astype(F32), axis=-1, keepdims=True)
            lse = lse_ref[s]
            pos = jnp.concatenate([qpos_ref[at, :]] * heads_q, axis=0)

            dq = jnp.zeros((q.shape[0], HEAD_SIZE), F32)
            for n in range(0, (s + 1) * groups, span):
                both = keys[n : n + span].reshape(span * block, 2 * HEAD_SIZE)
                key = both[:, :HEAD_SIZE]
                scores = dot_nt(q, key) * scale
                key_at = kpos_ref[:, n * block : (n + span) * block]
                scores = jnp.where(key_at <= pos, scores, MASKED)
                probs = jnp.exp(scores - lse)
                d_probs = dot_nt(grad, both[:, HEAD_SIZE:])
                d_scores = (probs * (d_probs - delta)).astype(BF)
                d_keys = dot_tn(d_scores, q) * scale
                d_values = dot_tn(probs.astype(BF), grad)
                both = jnp.concatenate([d_keys, d_values], axis=1)
                both = both.reshape(span, block, 2 * HEAD_SIZE)
                sums[n : n + span] = sums[n : n + span] + both
                dq = dq + dot(d_scores, key)
            dq = dq * scale
            for h in range(heads_q):
                lanes = slice(h * HEAD_SIZE, (h + 1) * HEAD_SIZE)
                d_raw, d_gain = rope_back(
                    dq[h * block : (h + 1) * block],
                    q_raw_ref[at, lanes],
                    gq_ref[...],
                    cos_ref[at, :],
                    sin_ref[at, :],
                )
                dq_ref[at, lanes] = d_raw.astype(BF)
                gain_total = gain_total + d_gain
        gain_out[...] = gain_total
        for mix, lane, sent_ref, kept_ref in (
            (key_mix, 0, k_sent, k_kept),
            (value_mix, HEAD_SIZE, v_sent, v_kept),
        ):
            for n, which in enumerate(mix):
                for s in range(segments):
                    value = sums[s * groups + slot[which], :, lane : lane + HEAD_SIZE].astype(BF)
                    rows_at = slice(s * block, (s + 1) * block)
                    if n < groups // 2:
                        kept_ref[n, rows_at, :] = value
                    else:
                        sent_ref[n - groups // 2, rows_at, :] = value
        heads = out_ref[...].astype(BF)
        for n, which in enumerate(out_mix):
            j = slot[which]
            value = dot_tn(heads, d_all_ref[:, j * chunk : (j + 1) * chunk]).astype(BF)
            for f in range(4):
                ref, at = (o_kept, n) if n < groups // 2 else (o_sent, n - groups // 2)
                lines = slice(f * piece, (f + 1) * piece)
                for b in range(0, wide_q, piece):
                    ref[at, lines, b : b + piece] = value[b : b + piece, lines]

    part_shape = ((groups // 2, all_rows, HEAD_SIZE), BF)
    o_shape = ((groups // 2, chunk, wide_q), BF)
    d_all, d_q, d_gain_q, k_sent, k_kept, v_sent, v_kept, o_sent, o_kept = call(
        attend_back,
        "attend_back",
        [
            ((all_rows, width), BF),
            ((all_rows, wide_q), BF),
            ((1, HEAD_SIZE), F32),
            part_shape,
            part_shape,
            part_shape,
            part_shape,
            o_shape,
            o_shape,
        ],
        [
            *d_parts,
            *kv_all,
            *o_parts,
            q,
            qpos,
            kpos,
            attended,
            lse,
            q_raw,
            cosine,
            sine,
            gain_q,
        ],
        ties=[out_sent],
        scratch=[
            pltpu.VMEM((segments * groups, block, 2 * HEAD_SIZE), BF),
            pltpu.VMEM((wide_q, width), BF),
            pltpu.VMEM((segments * groups, block, 2 * HEAD_SIZE), F32),
        ],
    )

    out_pair = reduce_to_pair(o_sent, o_kept, near, "r_out")

    with jax.named_scope("rs3"):
        out_sent, out_kept = add_split(out_kept, out_got, "rs3_t", [k_sent])
        out_kept, out_got = out_kept.reshape(own, width), swap(out_sent, SPLIT)
        out_got = out_got.reshape(own, width)
    d_keys = reduce_groups(k_sent, k_kept, near, "r_k")
    d_values = reduce_groups(v_sent, v_kept, far, "r_v")

    gate_up_sums = add_joined([gate_pair, up_pair], "sum_gu", [k_sent])
    gate_up = trade(gate_up_sums.reshape(4, piece, 2 * wide_f), "t_dgu")

    def key_back(dk_ref, dv_ref, raw_ref, cos_ref, sin_ref, gain_ref, out_ref, gain_out):
        d_raw, d_gain = rope_back(
            dk_ref[...], raw_ref[...], gain_ref[...], cos_ref[...], sin_ref[...]
        )
        out_ref[:, :HEAD_SIZE] = d_raw.astype(BF)
        out_ref[:, HEAD_SIZE:] = dv_ref[...].astype(BF)
        gain_out[...] = d_gain

    d_kv, d_gain_k = call(
        key_back,
        "key_back",
        [((all_rows, 2 * HEAD_SIZE), BF), ((1, HEAD_SIZE), F32)],
        [d_keys, d_values, k_raw, cosine, sine, gain_k],
        ties=[o_sent, out_sent, gate_up_sums],
    )

    def project_back(*refs):
        wq, wkv, refs = refs[:groups], refs[groups : 2 * groups], refs[2 * groups :]
        dq_ref, dkv_ref, x_ref, gain_ref, sent_ref, kept_ref, gain_out, *outs = refs
        for n, (g_ref, order) in enumerate(((dq_ref, near), (dkv_ref, far))):
            for at, which in enumerate(mix_list(order)):
                j = slot[which]
                value = dot_tn(x_ref[:, j * chunk : (j + 1) * chunk], g_ref[...]).astype(BF)
                if at < groups // 2:
                    outs[2 * n + 1][at] = value
                else:
                    outs[2 * n][at - groups // 2] = value
        for j in range(groups):
            lanes = slice(j * chunk, (j + 1) * chunk)
            gain_sum = jnp.zeros((1, chunk), F32)
            for s in range(segments):
                at = slice(s * block, (s + 1) * block)
                value = dot_nt(dq_ref[at, :], wq[j][...]) + dot_nt(dkv_ref[at, :], wkv[j][...])
                store_pair(sent_ref, kept_ref, s, value, j * chunk)
                gain_sum = gain_sum + jnp.sum(
                    value * x_ref[at, lanes].astype(F32), axis=0, keepdims=True
                )
            gain_out[:, lanes] = gain_sum / gain_ref[:, lanes]

    sent, kept, d_gain_a, q_sent, q_kept, kv_sent, kv_kept = call(
        project_back,
        "project_back",
        [
            *pair,
            (line_shape, F32),
            *[((groups // 2, chunk, wide_q), BF)] * 2,
            *[((groups // 2, chunk, 2 * HEAD_SIZE), BF)] * 2,
        ],
        [*q_parts, *kv_parts, d_q, d_kv, normed_all, gain_a],
    )
    with jax.named_scope("rs4"):
        got = swap(sent, CORE)
    with jax.named_scope("rs4"):
        sent, kept = add_split(kept, got, "rs4_c")
        got = swap_tp(sent)
    with jax.named_scope("rs4"):
        sent, kept = add_split(kept, got, "rs4_t")
        kept, got = kept.reshape(own, width), swap(sent, SPLIT).reshape(own, width)
    q_pair = reduce_to_pair(q_sent, q_kept, near, "r_q")
    kv_pair = reduce_to_pair(kv_sent, kv_kept, far, "r_kv")
    qkv_sums = add_joined([q_pair, kv_pair, out_pair], "sum_qkv", [sent, gate_up])
    qkv_sums = trade(qkv_sums.reshape(4, piece, qkv_sums.shape[1]), "t_dqkv").astype(F32)

    def join(value, start, stop):
        return jnp.concatenate([value[n, :, start:stop] for n in range(4)], axis=1)

    gate_up = gate_up.astype(F32)
    gate_grad = join(gate_up, 0, wide_f)
    up_grad = join(gate_up, wide_f, 2 * wide_f)
    query_grad = join(qkv_sums, 0, wide_q)
    key_grad = join(qkv_sums, wide_q, wide_q + HEAD_SIZE)
    value_grad = join(qkv_sums, wide_q + HEAD_SIZE, wide_q + 2 * HEAD_SIZE)
    output_grad = qkv_sums[:, :, wide_q + 2 * HEAD_SIZE :]
    output_grad = output_grad.reshape(4, piece, wide_q // piece, piece).transpose(0, 2, 1, 3)
    output_grad = output_grad.reshape(4 * wide_q, piece)

    layer_output = (middle + (out_kept.astype(F32) + out_got.astype(F32))).astype(BF)
    layer_output = put_back([layer_output], "leave1", [sent])[0].reshape(layer_input.shape)

    def last_back(kept_ref, got_ref, x_ref, gain_ref, d_ref, out_ref):
        grad = kept_ref[...].astype(F32) + got_ref[...].astype(F32)
        back, _ = norm_back(grad, x_ref[...].astype(F32), gain_ref[...])
        out_ref[...] = (d_ref[...] + back).astype(BF)

    (d_x,) = call(
        last_back,
        "norm1_back",
        [((own, width), BF)],
        [kept, got, x_own, gain_a, d_middle],
    )
    input_grad = put_back([d_x], "leave2")[0].reshape(layer_input.shape)

    d_gain_a, d_gain_m = put_back([d_gain_a, d_gain_m], "leave3", [got])
    gains = jnp.concatenate([d_gain_a, d_gain_m, d_gain_q, d_gain_k], axis=1).reshape(-1, 128)
    for bit in [CORE] + row_bits:
        gains = gains + swap(gains, bit)
    gains = gains + swap_tp(gains)
    gains = (gains + swap(gains, SPLIT)).reshape(-1)
    return (
        layer_output,
        input_grad,
        query_grad,
        key_grad,
        value_grad,
        output_grad,
        gate_grad,
        up_grad,
        down_grad,
        gains[:width],
        gains[width : 2 * width],
        gains[2 * width : 2 * width + HEAD_SIZE],
        gains[2 * width + HEAD_SIZE :],
    )


def solution(mesh):
    rows_in = P(None, "dp", "tp", None)
    in_specs = (
        rows_in,
        P("dp", "tp"),
        P("dp", "tp"),
        P("dp", "tp"),
        P("tp", "dp"),
        P("dp", "tp"),
        P("dp", "tp"),
        P("tp", "dp"),
        P(),
        P(),
        P(),
        P(),
        rows_in,
    )
    out_specs = (
        rows_in,
        rows_in,
        P("dp", "tp"),
        P("dp", "tp"),
        P("dp", "tp"),
        P("tp", "dp"),
        P("dp", "tp"),
        P("dp", "tp"),
        P("tp", "dp"),
        P(),
        P(),
        P(),
        P(),
    )
    return jax.shard_map(local, mesh=mesh, in_specs=in_specs, out_specs=out_specs, check_vma=False)
```
